512 devices in a mesh: vocab: 4 (over x), rows: 128 (over y, z, core).
Axes of the slice: x: 4, y: 8, z: 8, core: 2. Of those that a mesh axis runs over, the one named last changes fastest.
Arguments:
- hidden: bfloat16 [4, 4096, 8192], P(None, 'rows'), may hold values from -0.75 to 0.75
- teacher_weight: bfloat16 [8192, 1536], P('rows', 'vocab'), may hold values from -20 to 20
- draft_weight: bfloat16 [8192, 512], P('rows', 'vocab'), may hold values from -20 to 20
- draft_list: int32 [4, 4], replicated, may hold values from 0 to 11, as said below
Outputs:
- row_loss: float32 [4, 4096], P(None, 'rows')
- grad_hidden: bfloat16 [4, 4096, 8192], P(None, 'rows')
- grad_draft: float32 [8192, 512], P('rows', 'vocab')
The draws below stay inside these ranges and needn't reach their ends.
Inputs may be any that keep to these rules, and one draw needn't show every extreme that they name: `draft_list`: in each tile the 4 listed blocks are distinct.
All inputs are finite; a program needn't handle non-finite values.
Results may differ from the reference program's by a relative error of at most 0.008.
Values may be sent and summed in bfloat16 or wider, within the bound.
A program may use at most 64 MiB of HBM per device.

```python
import jax
import jax.numpy as jnp
from jax import lax

D = 8192
BLK = 128
TILES = 4
DS_DEV = 1
NFB = 12
NDS = 4
TILE_ROWS = 4096
VOCAB_FULL = 1536
VOCAB_DRAFT = 512
N_VOCAB = 4


def column_head(key, columns):
    normal_part = jnp.clip(jax.random.normal(jax.random.fold_in(key, 1), (D, columns), jnp.float32), -4.0, 4.0)
    scales = jnp.exp(jax.random.uniform(jax.random.fold_in(key, 2), (1, columns), jnp.float32, jnp.log(0.5), jnp.log(5.0)))
    return (normal_part * scales).astype(jnp.bfloat16)


def weight_pair(key):
    teacher_head = column_head(jax.random.fold_in(key, 101), VOCAB_FULL)
    draft_head = column_head(jax.random.fold_in(key, 202), VOCAB_DRAFT)
    return (teacher_head, draft_head)


def draw_teacher_weight(key, part):
    return weight_pair(key)[0]


def draw_draft_weight(key, part):
    return weight_pair(key)[1]


def draw_draft_list(key, part):
    shuffled = jax.random.permutation(jax.random.fold_in(key, 5), NFB)
    position = (jnp.arange(TILES)[:, None] * NDS + jnp.arange(NDS)[None, :]) % NFB
    return shuffled[position].astype(jnp.int32)


def draw_hidden(key, part):
    shape_all = (TILES, TILE_ROWS, D)
    row_scale = jnp.exp(jax.random.uniform(jax.random.fold_in(key, 11), (TILES, TILE_ROWS, 1), jnp.float32, jnp.log(0.3), jnp.log(3.0)))
    base_values = jnp.clip(jax.random.normal(jax.random.fold_in(key, 12), shape_all, jnp.float32), -4.0, 4.0)
    values_out = 0.011 * row_scale * base_values
    return jnp.clip(values_out, -0.75, 0.75).astype(jnp.bfloat16)


def setup_inputs(seed: int = 0) -> dict:
    key_of = jax.random.split(jax.random.key(seed), 5)
    return {
        "hidden": draw_hidden(jax.random.fold_in(key_of[4], 71), 0),
        "teacher_weight": draw_teacher_weight(jax.random.fold_in(key_of[4], 71), 0),
        "draft_weight": draw_draft_weight(jax.random.fold_in(key_of[4], 71), 0),
        "draft_list": draw_draft_list(jax.random.fold_in(key_of[4], 71), 0),
    }


def rounded(values):
    return lax.optimization_barrier(values.astype(jnp.bfloat16)).astype(jnp.float32)

def reference(hidden, teacher_weight, draft_weight, draft_list):
    losses = []
    hidden_grads = []
    weight_grad = jnp.zeros((D, VOCAB_DRAFT), jnp.float32)
    group_cols = DS_DEV * BLK
    for tile_index in range(TILES):
        tile_rows = hidden[tile_index]
        teacher_logits = jnp.dot(tile_rows.astype(jnp.float32), teacher_weight.astype(jnp.float32), preferred_element_type=jnp.float32)
        draft_logits = jnp.dot(tile_rows.astype(jnp.float32), draft_weight.astype(jnp.float32), preferred_element_type=jnp.float32)
        teacher_max = jnp.max(teacher_logits, axis=1, keepdims=True)
        teacher_total = jnp.sum(jnp.exp(teacher_logits - teacher_max), axis=1, keepdims=True)
        blocks = teacher_logits.reshape(TILE_ROWS, NFB, BLK)
        picked = jnp.take(blocks, draft_list[tile_index].astype(jnp.int32), axis=1).reshape(TILE_ROWS, VOCAB_DRAFT)
        target = jnp.exp(picked - teacher_max) / teacher_total
        covered = jnp.sum(target, axis=1, keepdims=True)
        draft_max = jnp.max(draft_logits, axis=1, keepdims=True)
        draft_total = jnp.sum(jnp.exp(draft_logits - draft_max), axis=1, keepdims=True)
        log_prob = draft_logits - draft_max - jnp.log(draft_total)
        losses.append(-jnp.sum(target * log_prob, axis=1))
        draft_prob = jnp.exp(draft_logits - draft_max) / draft_total
        logit_grad = (covered * draft_prob - target).astype(jnp.bfloat16)
        summed = jnp.zeros((TILE_ROWS, D), jnp.float32)
        for group_index in range(N_VOCAB):
            lower_col = group_index * group_cols
            partial_value = lax.dot_general(logit_grad[:, lower_col:lower_col + group_cols].astype(jnp.float32), draft_weight[:, lower_col:lower_col + group_cols].astype(jnp.float32), (((1,), (1,)), ((), ())), preferred_element_type=jnp.float32)
            summed = summed + rounded(partial_value)
        hidden_grads.append(summed.astype(jnp.bfloat16))
        weight_grad = weight_grad + lax.dot_general(tile_rows.astype(jnp.float32), logit_grad.astype(jnp.float32), (((0,), (0,)), ((), ())), preferred_element_type=jnp.float32)
    return (jnp.stack(losses), jnp.stack(hidden_grads), weight_grad)
```

```python
import functools
import heapq

import jax
import jax.numpy as jnp
from jax import lax
from jax.experimental import pallas as pl
from jax.experimental.pallas import tpu as pltpu
from jax.sharding import PartitionSpec as P

BLK = 128
F32 = jnp.float32
BF16 = jnp.bfloat16
MESH = pl.DeviceIdType.MESH
NT = (((1,), (1,)), ((), ()))


def offset_of(k):
    return 0 if k == 0 else (-(k + 1) // 2 if k % 2 else k // 2)


def reach(ring, kind, k):
    half = ring // 2
    if kind == "P" or k % 2 == 0:
        return {"R": half, "L": half - 1}
    return {"R": half - 1, "L": half}


def follow(ring, event):
    kind, k, way, dist = event
    sends = []
    if kind == "P":
        if way is None:
            sends += [("P", 0, w, 1) for w in "RL" if reach(ring, "P", 0)[w] >= 1]
            first = 0
        else:
            if dist < reach(ring, "P", 0)[way]:
                sends.append(("P", 0, way, dist + 1))
            first = 2 * dist - 1 if way == "R" else 2 * dist
        sends += [("Q", first, w, 1) for w in "RL" if reach(ring, "Q", first)[w] >= 1]
    elif dist < reach(ring, "Q", k)[way]:
        sends.append(("Q", k, way, dist + 1))
    return sends


def event_order(ring, slab_us=0.7, hop_us=1.7, step_us=0.2):
    free = {"R": 0.0, "L": 0.0}
    arrivals, order, now, count = [], [], 0.0, 0
    pending = [("P", 0, None, 0)]
    while True:
        for event in pending:
            for sent in follow(ring, event):
                way = sent[2]
                free[way] = max(free[way], now) + slab_us
                count += 1
                heapq.heappush(arrivals, (free[way] + hop_us, count, sent))
        if not arrivals:
            return order
        when, _, event = heapq.heappop(arrivals)
        now = max(now + step_us, when)
        order.append(event)
        pending = [event]


def kernel(
    nx, ring, list_ref, hid_ref, tw_ref, dw_ref, loss_ref, gh_ref, gd_ref,
    wbuf, hb, acc, full, dall, msg, msgr, eown, lgall, crs, crsr, rss, rsr, rso, fsd, fin, ghs,
    init_sem, hid_sem, ag_send, ag_recv, xg_send, xg_recv, xr_send, lx_send, lx_recv, sm_send, sm_recv,
    lg_send, lg_recv, cr_send, cr_recv, rs_send, rs_recv, f_send, f_recv, gh_send, gh_recv, gh_loc,
):
    x = lax.axis_index("vocab")
    r = lax.axis_index("rows")
    c = lax.rem(r, 2)
    chip = r // 2
    y, z = chip // ring, lax.rem(chip, ring)
    p = y + c * (z - y)
    q = z + c * (y - z)
    half = ring // 2

    def mod(v):
        return lax.rem(v + 2 * ring, ring)

    def xmod(v):
        return lax.rem(v + nx, nx)

    def chip_of(pp, qq):
        straight, turned = pp * ring + qq, qq * ring + pp
        return straight + c * (turned - straight)

    def at(pp, qq):
        return (x, chip_of(mod(pp), mod(qq)) * 2 + c)

    partner = (x, chip * 2 + 1 - c)

    def rcopy(src, dst, ssem, rsem, dev):
        return pltpu.make_async_remote_copy(
            src_ref=src, dst_ref=dst, send_sem=ssem, recv_sem=rsem, device_id=dev, device_id_type=MESH
        )

    hid_local = pltpu.make_async_copy(hid_ref, hb.at[0:128], hid_sem.at[0])
    own = wbuf.at[p, q]
    loc_a0 = pltpu.make_async_copy(tw_ref.at[:, 0:256], own.at[0:64, :], init_sem.at[0])
    loc_b1 = pltpu.make_async_copy(tw_ref.at[:, 256:384], own.at[64:128, 0:128], init_sem.at[0])
    loc_b2 = pltpu.make_async_copy(dw_ref, own.at[64:128, 128:256], init_sem.at[1])

    @pl.when(c == 0)
    def _():
        loc_a0.start()

    @pl.when(c == 1)
    def _():
        loc_b1.start()
        loc_b2.start()

    hid_local.start()

    barrier = pltpu.get_barrier_semaphore()
    greeted = 0
    for d in range(1, ring):
        for core in (0, 1):
            for dev in ((mod(y + d) * ring + z), (y * ring + mod(z + d))):
                pl.semaphore_signal(barrier, inc=1, device_id=(x, dev * 2 + core), device_id_type=MESH)
                greeted += 1
    for d in range(1, nx):
        for core in (0, 1):
            pl.semaphore_signal(barrier, inc=1, device_id=(xmod(x + d), chip * 2 + core), device_id_type=MESH)
            greeted += 1
    pl.semaphore_signal(barrier, inc=1, device_id=partner, device_id_type=MESH)
    pl.semaphore_wait(barrier, greeted + 1)

    there = wbuf.at[q, p]
    to_b1 = rcopy(tw_ref.at[:, 256:384], there.at[0:64, 0:128], init_sem.at[2], init_sem.at[4], partner)
    to_b2 = rcopy(dw_ref, there.at[0:64, 128:256], init_sem.at[3], init_sem.at[5], partner)
    to_a = rcopy(tw_ref.at[:, 0:256], there.at[64:128, :], init_sem.at[2], init_sem.at[4], partner)
    from_a1 = rcopy(tw_ref.at[:, 256:384], own.at[0:64, 0:128], init_sem.at[2], init_sem.at[4], partner)
    from_a2 = rcopy(dw_ref, own.at[0:64, 128:256], init_sem.at[3], init_sem.at[5], partner)
    from_b = rcopy(tw_ref.at[:, 0:256], own.at[64:128, :], init_sem.at[2], init_sem.at[4], partner)

    @pl.when(c == 0)
    def _():
        to_b1.start()
        to_b2.start()

    @pl.when(c == 1)
    def _():
        to_a.start()

    hid_out = rcopy(hid_ref, hb.at[128:256], hid_sem.at[1], hid_sem.at[2], partner)
    hid_out.start()

    @pl.when(c == 0)
    def _():
        loc_a0.wait()
        from_b.wait_recv()

    @pl.when(c == 1)
    def _():
        loc_b1.wait()
        loc_b2.wait()
        from_a1.wait_recv()
        from_a2.wait_recv()

    events = event_order(ring)
    number = {event: i for i, event in enumerate(events)}

    def slab_pos(event):
        kind, k, way, dist = event
        step = -dist if way == "R" else dist
        if kind == "P":
            return mod(p + step), q
        return mod(p + offset_of(k)), mod(q + step)

    def send_along(sent, pos):
        kind, _, way, _ = sent
        step = 1 if way == "R" else -1
        dev = at(p + step, q) if kind == "P" else at(p, q + step)
        i = number[sent]
        slab = wbuf.at[pos[0], pos[1]]
        rcopy(slab, slab, ag_send.at[i], ag_recv.at[i], dev).start()

    def multiply(pos):
        pp, qq = pos
        lanes = pl.ds(pl.multiple_of(chip_of(pp, qq) * 128, 128), 128)
        acc[...] += jnp.dot(hb[:, lanes], wbuf[pp, qq], preferred_element_type=F32)

    def class_of(event):
        kind, k, way, dist = event
        if kind == "P":
            return (0, 0)
        if dist == half:
            return (1, half - 1)
        return (0, dist) if way == "L" else (1, dist - 1)

    left_in_class = {}
    for event in events:
        left_in_class[class_of(event)] = left_in_class.get(class_of(event), 0) + 1

    def class_q(h, i):
        return mod(q + i) if h == 0 else mod(q - 1 - i)

    def x_copies(h, i):
        src = wbuf.at[:, class_q(h, i), :, 128:256]
        dst = dall.at[x, i]
        out = []
        if nx > 1:
            out.append(rcopy(src, dst, xg_send.at[h, i, 0], xg_recv.at[0, i], (xmod(x + 1), chip * 2 + h)))
            out.append(rcopy(src, dst, xg_send.at[h, i, 1], xg_recv.at[1, i], (xmod(x - 1), chip * 2 + h)))
        if h == 0:
            out.append(rcopy(src, dst, xg_send.at[h, i, 2], xg_recv.at[3, i], (x, chip * 2)))
        else:
            out.append(pltpu.make_async_copy(src, dst, xg_recv.at[3, i]))
        return out

    def x_start(h, i):
        @pl.when(c == 1)
        def _():
            for copy in x_copies(h, i):
                copy.start()

    def x_arrived(kind, i):
        group = {0: xmod(x - 1), 1: xmod(x + 1), 2: xmod(x + 2), 3: x}[kind]
        slot = dall.at[group, i]
        return rcopy(slot, slot, xr_send.at[i], xg_recv.at[kind, i], (xmod(x + 1), r))

    def x_relay(i):
        if nx == 4:
            kind = i % 2
            x_arrived(kind, i).wait_recv()
            group = xmod(x - 1) if kind == 0 else xmod(x + 1)
            dev = (xmod(x + 1), r) if kind == 0 else (xmod(x - 1), r)
            slot = dall.at[group, i]
            rcopy(slot, slot, xr_send.at[i], xg_recv.at[2, i], dev).start()

    for sent in follow(ring, ("P", 0, None, 0)):
        send_along(sent, (p, q))
    acc[...] = jnp.zeros_like(acc)

    todo = [(p, q)]
    have_hidden = False
    held = []
    ready = []
    relayed = 0
    for n, event in enumerate(events):
        pos = slab_pos(event)
        slab = wbuf.at[pos[0], pos[1]]
        rcopy(slab, slab, ag_send.at[n], ag_recv.at[n], partner).wait_recv()
        for sent in follow(ring, event):
            send_along(sent, pos)
        cls = class_of(event)
        left_in_class[cls] -= 1
        if left_in_class[cls] == 0:
            if n < 0.7 * len(events):
                x_start(*cls)
                ready.append((cls[1], n))
            else:
                held.append(cls)
        if relayed < half and n >= 20:
            both = [m for i, m in ready if i == relayed]
            if len(both) == 2 and n >= max(both) + 12:
                x_relay(relayed)
                relayed += 1
        todo.append(pos)
        if n >= min(10, len(events) - 1):
            if not have_hidden:
                hid_local.wait()
                hid_out.wait_recv()
                have_hidden = True
            for _ in range(min(2, len(todo))):
                multiply(todo.pop(0))
    for pos in todo:
        multiply(pos)

    cols = pl.ds(pl.multiple_of(c * 256, 256), 256)
    lx = rcopy(acc.at[128:256], full.at[:, cols], lx_send, lx_recv, partner)
    lx.start()
    full[:, cols] = acc[0:128, :]
    other = full.at[:, pl.ds(pl.multiple_of((1 - c) * 256, 256), 256)]
    rcopy(other, other, lx_send, lx_recv, partner).wait_recv()

    t_logits = full[:, 0:384]
    d_logits = full[:, 384:512]
    t_max = jnp.max(t_logits, axis=1, keepdims=True)
    t_exp = jnp.exp(t_logits - t_max)
    t_sum = jnp.sum(t_exp, axis=1, keepdims=True)
    d_max = jnp.max(d_logits, axis=1, keepdims=True)
    d_sum = jnp.sum(jnp.exp(d_logits - d_max), axis=1, keepdims=True)
    covers = []
    for t in range(4):
        rows = slice(32 * t, 32 * t + 32)
        total = jnp.zeros((32, 128), F32)
        for d in range(nx):
            wanted = list_ref[t, xmod(x + d)]
            piece = jnp.zeros((32, 128), F32)
            for b in range(3):
                keep = jnp.where(wanted == 3 * x + b, 1.0, 0.0).astype(F32)
                piece += keep * t_exp[rows, 128 * b:128 * b + 128]
            if d == 0:
                eown[rows, :] = piece
            else:
                msg[d - 1, rows, :] = piece
            total += piece
        covers.append(jnp.sum(total, axis=1, keepdims=True))
    cover = jnp.concatenate(covers, axis=0)
    lane = lax.broadcasted_iota(jnp.int32, (128, 128), 1)
    stats = jnp.zeros((128, 128), F32)
    for i, value in enumerate((t_max, t_sum, cover, d_max, d_sum)):
        stats = jnp.where(lane == i, value, stats)
    stats_row = stats.T[0:8, :]
    for d in range(1, nx):
        msg[d - 1, 128:136, :] = stats_row

    def sm_copy(d):
        return rcopy(msg.at[d - 1], msgr.at[d - 1], sm_send.at[d - 1], sm_recv.at[d - 1], (xmod(x + d), r))

    for d in range(1, nx):
        sm_copy(d).start()
    for cls in held:
        x_start(*cls)
    for d in range(1, nx):
        sm_copy(d).wait_recv()
    stat = [(t_max, t_sum, cover, d_max, d_sum)]
    for d in range(1, nx):
        got = jnp.concatenate([msgr[d - 1, 128:136, :]] * 16, axis=0).T
        stat.append(tuple(got[:, i:i + 1] for i in range(5)))
    all_tmax = functools.reduce(jnp.maximum, [s[0] for s in stat])
    all_dmax = functools.reduce(jnp.maximum, [s[3] for s in stat])
    t_scale = [jnp.exp(s[0] - all_tmax) for s in stat]
    all_tsum = sum(s[1] * a for s, a in zip(stat, t_scale))
    all_dsum = sum(s[4] * jnp.exp(s[3] - all_dmax) for s in stat)
    covered = sum(s[2] * a for s, a in zip(stat, t_scale)) / all_tsum
    target = eown[...] * (t_scale[0] / all_tsum)
    for d in range(1, nx):
        target += msgr[d - 1, 0:128, :] * (t_scale[d] / all_tsum)
    prob = jnp.exp(d_logits - all_dmax) / all_dsum
    lgall[x, 0:128, :] = (covered * prob - target).astype(BF16)

    def lg_copies():
        src = lgall.at[x, 0:128]
        out = [rcopy(src, lgall.at[x, 128:256], lg_send.at[0, 1], lg_recv.at[0, 1], partner)]
        for d in range(1, nx):
            xx = xmod(x + d)
            out.append(rcopy(src, lgall.at[x, 0:128], lg_send.at[d, 0], lg_recv.at[d, 0], (xx, r)))
            out.append(
                rcopy(src, lgall.at[x, 128:256], lg_send.at[d, 1], lg_recv.at[d, 1], (xx, chip * 2 + 1 - c))
            )
        return out

    def lg_wait(d, side):
        group = xmod(x - d)
        slot = lgall.at[group, 128 * side:128 * side + 128]
        rcopy(slot, slot, lg_send.at[d, side], lg_recv.at[d, side], partner).wait_recv()

    for copy in lg_copies():
        copy.start()
    crossed = jnp.sum(target * d_logits, axis=1, keepdims=True)
    crs[...] = jnp.broadcast_to(crossed, (128, 128)).T[0:8, :]

    def cr_copy(d):
        return rcopy(crs, crsr.at[d - 1], cr_send.at[d - 1], cr_recv.at[d - 1], (xmod(x + d), r))

    for d in range(1, nx):
        cr_copy(d).start()

    lg_wait(0, 1)
    lg_t = lgall[x].astype(F32).T.astype(BF16)
    odd = lax.rem(p + q + c, 2)

    def partial(pp, i):
        qq = 2 * i + lax.rem(pp + c, 2)
        lanes = pl.ds(pl.multiple_of(chip_of(pp, qq) * 128, 128), 128)
        return jnp.dot(lg_t, hb[:, lanes], preferred_element_type=F32)

    def rs_copy(d):
        return rcopy(rss.at[d - 1], rsr.at[d - 1], rs_send.at[d - 1], rs_recv.at[d - 1], at(p + d, q))

    for d in sorted(range(1, ring), key=lambda d: -min(d, ring - d)):
        for i in range(half):
            rss[d - 1, i] = partial(mod(p + d), i).astype(BF16)
        rs_copy(d).start()
    for i in range(half):
        rso[i] = partial(p, i)

    for i in range(relayed, half):
        x_relay(i)
    loss = covered * (all_dmax + jnp.log(all_dsum))
    loss_row = jnp.broadcast_to(loss, (128, 128)).T[0:8, :] - crs[...]
    for d in range(1, nx):
        cr_copy(d).wait_recv()
        loss_row -= crsr[d - 1]
    loss_ref[...] = loss_row

    for d in range(1, nx):
        for side in (0, 1):
            lg_wait(d, side)

    wide = ring * 128

    def gh_copies(i):
        qq = mod(q + i) if False else None
        yy = mod(y + i - c * (1 + 2 * i))
        lanes = pl.ds(pl.multiple_of(yy * wide, wide), wide)
        mine = pltpu.make_async_copy(ghs.at[i, 0:128], gh_ref.at[:, lanes], gh_loc.at[i])
        theirs = rcopy(ghs.at[i, 128:256], gh_ref.at[:, lanes], gh_send.at[i], gh_recv.at[i], partner)
        return mine, theirs

    for i in range(half):
        if nx > 1:
            for kind in (0, 1, 2):
                if kind == i % 2 or (kind == 2 and nx != 4):
                    continue
                x_arrived(kind, i).wait_recv()

        @pl.when(c == 0)
        def _():
            x_arrived(3, i).wait_recv()

        @pl.when(c == 1)
        def _():
            pltpu.make_async_copy(wbuf.at[:, class_q(1, i), :, 128:256], dall.at[x, i], xg_recv.at[3, i]).wait()

        def width(s, carry):
            summed = jnp.zeros((256, 128), F32)
            for g in range(nx):
                piece = lax.dot_general(lgall[g], dall[g, i, s], NT, preferred_element_type=F32)
                summed += piece.astype(BF16).astype(F32)
            ghs[i, :, pl.ds(pl.multiple_of(s * 128, 128), 128)] = summed.astype(BF16)
            return carry

        lax.fori_loop(0, ring, width, 0)
        for copy in gh_copies(i):
            copy.start()

    for d in range(1, ring):
        rs_copy(d).wait_recv()

    def add_up(i, carry):
        total = rso[i]
        for d in range(1, ring):
            total += rsr[d - 1, i].astype(F32)
        fsd[i] = total.T
        return carry

    lax.fori_loop(0, half, add_up, 0)

    def f_copy(i, core):
        d = odd + 2 * i
        qq = mod(q + d)
        j = (qq - lax.rem(p + c, 2)) // 2
        dev = (x, chip_of(p, qq) * 2 + core)
        return rcopy(
            fsd.at[j, 64 * core:64 * core + 64], fin.at[d], f_send.at[i, core], f_recv.at[d], dev
        )

    def f_stays(i, core):
        return jnp.logical_and(odd + 2 * i == 0, core == c)

    for i in range(half):
        for core in (0, 1):
            stays = f_stays(i, core)

            @pl.when(jnp.logical_not(stays))
            def _():
                f_copy(i, core).start()

            @pl.when(stays)
            def _():
                j = (q - lax.rem(p + c, 2)) // 2
                fin[0] = fsd[j, 64 * core:64 * core + 64, :]

    home = lax.rem(y + z + c, 2) == 0
    grad = jnp.zeros((64, 128), F32)
    for d in range(ring):
        slot = fin.at[d]
        arrival = rcopy(slot, slot, f_send.at[0, 0], f_recv.at[d], partner)
        if d == 0:
            pl.when(jnp.logical_not(home))(arrival.wait_recv)
        else:
            arrival.wait_recv()
        grad += fin[d]
    gd_ref[...] = grad

    for i in range(half):
        mine, theirs = gh_copies(i)
        mine.wait()
        theirs.wait_send()
    for i in range(half):
        mine, theirs = gh_copies(i)
        theirs.wait_recv()
    for i in range(half):
        for core in (0, 1):
            @pl.when(jnp.logical_not(f_stays(i, core)))
            def _():
                f_copy(i, core).wait_send()
    for d in range(1, ring):
        rs_copy(d).wait_send()
    for d in range(1, nx):
        cr_copy(d).wait_send()
        sm_copy(d).wait_send()
    for copy in lg_copies():
        copy.wait_send()
    lx.wait_send()
    hid_out.wait_send()

    @pl.when(c == 0)
    def _():
        to_b1.wait_send()
        to_b2.wait_send()

    @pl.when(c == 1)
    def _():
        to_a.wait_send()
        for h in (0, 1):
            for i in range(half):
                for n, copy in enumerate(x_copies(h, i)):
                    if nx > 1 and n < 2 or h == 0:
                        copy.wait_send()

    if nx == 4:
        for i in range(half):
            x_arrived(0, i).wait_send()
    for n, event in enumerate(events):
        slab = wbuf.at[0, 0]
        rcopy(slab, slab, ag_send.at[n], ag_recv.at[n], partner).wait_send()


def per_device(nx, ring, hidden, teacher_weight, draft_weight, draft_list):
    tiles, tile_rows, width = hidden.shape
    rows = tiles * tile_rows
    half = ring // 2
    dma = pltpu.SemaphoreType.DMA
    more = max(nx - 1, 1)
    scratch = [
        pltpu.VMEM((ring, ring, 128, 256), BF16),
        pltpu.VMEM((2 * rows, width), BF16),
        pltpu.VMEM((2 * rows, 256), F32),
        pltpu.VMEM((rows, 512), F32),
        pltpu.VMEM((nx, half, ring, 128, 128), BF16),
        pltpu.VMEM((more, rows + 8, 128), F32),
        pltpu.VMEM((more, rows + 8, 128), F32),
        pltpu.VMEM((rows, 128), F32),
        pltpu.VMEM((nx, 2 * rows, 128), BF16),
        pltpu.VMEM((8, 128), F32),
        pltpu.VMEM((more, 8, 128), F32),
        pltpu.VMEM((ring - 1, half, 128, 128), BF16),
        pltpu.VMEM((ring - 1, half, 128, 128), BF16),
        pltpu.VMEM((half, 128, 128), F32),
        pltpu.VMEM((half, 128, 128), F32),
        pltpu.VMEM((ring, 64, 128), F32),
        pltpu.VMEM((half, 2 * rows, ring * 128), BF16),
        dma((6,)), dma((3,)), dma((ring * ring,)), dma((ring * ring,)),
        dma((2, half, 3)), dma((4, half)), dma((half,)),
        dma(()), dma(()), dma((more,)), dma((more,)),
        dma((nx, 2)), dma((nx, 2)), dma((more,)), dma((more,)),
        dma((ring - 1,)), dma((ring - 1,)), dma((half, 2)), dma((ring,)),
        dma((half,)), dma((half,)), dma((half,)),
    ]
    hbm = pl.BlockSpec(memory_space=pl.ANY)
    vmem = pl.BlockSpec(memory_space=pltpu.VMEM)
    loss, grad_hidden, grad_draft = pl.pallas_call(
        functools.partial(kernel, nx, ring),
        out_shape=(
            jax.ShapeDtypeStruct((8, 128), F32),
            jax.ShapeDtypeStruct((rows, width), BF16),
            jax.ShapeDtypeStruct((64, 128), F32),
        ),
        in_specs=[pl.BlockSpec(memory_space=pltpu.SMEM), hbm, hbm, hbm],
        out_specs=(vmem, hbm, vmem),
        scratch_shapes=scratch,
        compiler_params=pltpu.CompilerParams(
            collective_id=0, has_side_effects=True, vmem_limit_bytes=48 * 1024 * 1024
        ),
        name="distill",
    )(draft_list, hidden.reshape(rows, width), teacher_weight, draft_weight)
    return loss[0].reshape(tiles, tile_rows), grad_hidden.reshape(hidden.shape), grad_draft


def solution(mesh):
    nx, devices = mesh.shape["vocab"], mesh.shape["rows"]
    ring = int(round((devices // 2) ** 0.5))
    in_specs = (P(None, "rows", None), P("rows", "vocab"), P("rows", "vocab"), P())
    out_specs = (P(None, "rows"), P(None, "rows", None), P("rows", "vocab"))
    return jax.shard_map(
        functools.partial(per_device, nx, ring), mesh=mesh, in_specs=in_specs, out_specs=out_specs, check_vma=False
    )
```

```python
import functools
import heapq

import jax
import jax.numpy as jnp
from jax import lax
from jax.experimental import pallas as pl
from jax.experimental.pallas import tpu as pltpu
from jax.sharding import PartitionSpec as P

CHUNKS = 8
F32 = jnp.float32
BF16 = jnp.bfloat16
MESH = pl.DeviceIdType.MESH
NT = (((1,), (1,)), ((), ()))


def offset_of(k):
    return 0 if k == 0 else (-(k + 1) // 2 if k % 2 else k // 2)


def reach(ring, kind, k):
    half = ring // 2
    if kind == "P" or k % 2 == 0:
        return {"R": half, "L": half - 1}
    return {"R": half - 1, "L": half}


def follow(ring, event):
    kind, k, way, dist = event
    sends = []
    if kind == "P":
        if way is None:
            sends += [("P", 0, w, 1) for w in "RL" if reach(ring, "P", 0)[w] >= 1]
            first = 0
        else:
            if dist < reach(ring, "P", 0)[way]:
                sends.append(("P", 0, way, dist + 1))
            first = 2 * dist - 1 if way == "R" else 2 * dist
        sends += [("Q", first, w, 1) for w in "RL" if reach(ring, "Q", first)[w] >= 1]
    elif dist < reach(ring, "Q", k)[way]:
        sends.append(("Q", k, way, dist + 1))
    return sends


def event_order(ring, slab_us=0.7, hop_us=1.7, step_us=0.2):
    free = {"R": 0.0, "L": 0.0}
    arrivals, order, now, count = [], [], 0.0, 0
    pending = [("P", 0, None, 0)]
    while True:
        for event in pending:
            for sent in follow(ring, event):
                way = sent[2]
                free[way] = max(free[way], now) + slab_us
                count += 1
                heapq.heappush(arrivals, (free[way] + hop_us, count, sent))
        if not arrivals:
            return order
        when, _, event = heapq.heappop(arrivals)
        now = max(now + step_us, when)
        order.append(event)
        pending = [event]


def kernel(
    nx, ring, list_ref, hid_ref, tw_ref, dw_ref, loss_ref, gh_ref, gd_ref,
    wbuf, hb, acc, full, dall, dq, msg, msgr, eown, lgall, crs, crsr, rss, rsr, rso, fsd, fin, ghs,
    init_sem, hid_sem, ag_send, ag_recv, xg_send, xg_recv, xr_send, dq_send, dq_recv, lx_send, lx_recv, sm_send, sm_recv,
    lg_send, lg_recv, cr_send, cr_recv, rs_send, rs_recv, f_send, f_recv, gh_send, gh_recv, gh_loc,
    gx_send, gx_recv, gy_send,
):
    x = lax.axis_index("vocab")
    r = lax.axis_index("rows")
    c = lax.rem(r, 2)
    chip = r // 2
    y, z = chip // ring, lax.rem(chip, ring)
    p = y + c * (z - y)
    q = z + c * (y - z)
    half = ring // 2
    whole = half // 2
    part = ring // nx

    def mod(v):
        return lax.rem(v + 2 * ring, ring)

    def xmod(v):
        return lax.rem(v + nx, nx)

    def chip_of(pp, qq):
        straight, turned = pp * ring + qq, qq * ring + pp
        return straight + c * (turned - straight)

    def at(pp, qq):
        return (x, chip_of(mod(pp), mod(qq)) * 2 + c)

    partner = (x, chip * 2 + 1 - c)

    def rcopy(src, dst, ssem, rsem, dev):
        return pltpu.make_async_remote_copy(
            src_ref=src, dst_ref=dst, send_sem=ssem, recv_sem=rsem, device_id=dev, device_id_type=MESH
        )

    hid_local = pltpu.make_async_copy(hid_ref, hb.at[0:128], hid_sem.at[0])
    own = wbuf.at[p, q]
    loc_a0 = pltpu.make_async_copy(tw_ref.at[:, 0:256], own.at[0:64, :], init_sem.at[0])
    loc_b1 = pltpu.make_async_copy(tw_ref.at[:, 256:384], own.at[64:128, 0:128], init_sem.at[0])
    loc_b2 = pltpu.make_async_copy(dw_ref, own.at[64:128, 128:256], init_sem.at[1])

    @pl.when(c == 0)
    def _():
        loc_a0.start()

    @pl.when(c == 1)
    def _():
        loc_b1.start()
        loc_b2.start()

    hid_local.start()

    barrier = pltpu.get_barrier_semaphore()
    greeted = 0
    for d in range(1, ring):
        for core in (0, 1):
            for dev in ((mod(y + d) * ring + z), (y * ring + mod(z + d))):
                pl.semaphore_signal(barrier, inc=1, device_id=(x, dev * 2 + core), device_id_type=MESH)
                greeted += 1
    for d in range(1, nx):
        for core in (0, 1):
            pl.semaphore_signal(barrier, inc=1, device_id=(xmod(x + d), chip * 2 + core), device_id_type=MESH)
            greeted += 1
    pl.semaphore_signal(barrier, inc=1, device_id=partner, device_id_type=MESH)
    pl.semaphore_wait(barrier, greeted + 1)

    there = wbuf.at[q, p]
    to_b1 = rcopy(tw_ref.at[:, 256:384], there.at[0:64, 0:128], init_sem.at[2], init_sem.at[4], partner)
    to_b2 = rcopy(dw_ref, there.at[0:64, 128:256], init_sem.at[3], init_sem.at[5], partner)
    to_a = rcopy(tw_ref.at[:, 0:256], there.at[64:128, :], init_sem.at[2], init_sem.at[4], partner)
    from_a1 = rcopy(tw_ref.at[:, 256:384], own.at[0:64, 0:128], init_sem.at[2], init_sem.at[4], partner)
    from_a2 = rcopy(dw_ref, own.at[0:64, 128:256], init_sem.at[3], init_sem.at[5], partner)
    from_b = rcopy(tw_ref.at[:, 0:256], own.at[64:128, :], init_sem.at[2], init_sem.at[4], partner)

    @pl.when(c == 0)
    def _():
        to_b1.start()
        to_b2.start()

    @pl.when(c == 1)
    def _():
        to_a.start()

    hid_out = rcopy(hid_ref, hb.at[128:256], hid_sem.at[1], hid_sem.at[2], partner)
    hid_out.start()

    @pl.when(c == 0)
    def _():
        loc_a0.wait()
        from_b.wait_recv()

    @pl.when(c == 1)
    def _():
        loc_b1.wait()
        loc_b2.wait()
        from_a1.wait_recv()
        from_a2.wait_recv()

    events = event_order(ring)
    number = {event: i for i, event in enumerate(events)}

    def slab_pos(event):
        kind, k, way, dist = event
        step = -dist if way == "R" else dist
        if kind == "P":
            return mod(p + step), q
        return mod(p + offset_of(k)), mod(q + step)

    def send_along(sent, pos):
        kind, _, way, _ = sent
        step = 1 if way == "R" else -1
        dev = at(p + step, q) if kind == "P" else at(p, q + step)
        i = number[sent]
        slab = wbuf.at[pos[0], pos[1]]
        rcopy(slab, slab, ag_send.at[i], ag_recv.at[i], dev).start()

    def multiply(pos):
        pp, qq = pos
        lanes = pl.ds(pl.multiple_of(chip_of(pp, qq) * 128, 128), 128)
        acc[...] += jnp.dot(hb[:, lanes], wbuf[pp, qq], preferred_element_type=F32)

    def class_of(event):
        kind, k, way, dist = event
        if kind == "P":
            return (0, 0)
        if dist == half:
            return (1, half - 1)
        return (0, dist) if way == "L" else (1, dist - 1)

    left_in_class = {}
    for event in events:
        left_in_class[class_of(event)] = left_in_class.get(class_of(event), 0) + 1

    def class_q(h, i):
        return mod(q + i) if h == 0 else mod(q - 1 - i)

    def x_copies(h, i):
        src = wbuf.at[:, class_q(h, i), :, 128:256]
        dst = dall.at[x, i]
        out = []
        if nx > 1:
            out.append(rcopy(src, dst, xg_send.at[h, i, 0], xg_recv.at[0, i], (xmod(x + 1), chip * 2 + h)))
            out.append(rcopy(src, dst, xg_send.at[h, i, 1], xg_recv.at[1, i], (xmod(x - 1), chip * 2 + h)))
        if h == 0:
            out.append(rcopy(src, dst, xg_send.at[h, i, 2], xg_recv.at[3, i], (x, chip * 2)))
        else:
            out.append(pltpu.make_async_copy(src, dst, xg_recv.at[3, i]))
        return out

    def dq_copies(h, i):
        out = []
        for d in range(nx):
            xx = xmod(x + d)
            src = wbuf.at[pl.ds(part * xx, part), class_q(h, i), :, 128:256]
            dst = dq.at[x, i - whole]
            if d == 0 and h == 1:
                out.append(pltpu.make_async_copy(src, dst, dq_recv.at[0, i - whole]))
            else:
                dev = (xx, chip * 2 + h)
                out.append(rcopy(src, dst, dq_send.at[h, i - whole, d], dq_recv.at[d, i - whole], dev))
        return out

    def x_start(h, i):
        @pl.when(c == 1)
        def _():
            for copy in x_copies(h, i) if i < whole else dq_copies(h, i):
                copy.start()

    def x_arrived(kind, i):
        group = {0: xmod(x - 1), 1: xmod(x + 1), 2: xmod(x + 2), 3: x}[kind]
        slot = dall.at[group, i]
        return rcopy(slot, slot, xr_send.at[i], xg_recv.at[kind, i], (xmod(x + 1), r))

    def x_relay(i):
        if nx == 4:
            kind = i % 2
            x_arrived(kind, i).wait_recv()
            group = xmod(x - 1) if kind == 0 else xmod(x + 1)
            dev = (xmod(x + 1), r) if kind == 0 else (xmod(x - 1), r)
            slot = dall.at[group, i]
            rcopy(slot, slot, xr_send.at[i], xg_recv.at[2, i], dev).start()

    for sent in follow(ring, ("P", 0, None, 0)):
        send_along(sent, (p, q))
    acc[...] = jnp.zeros_like(acc)

    todo = [(p, q)]
    have_hidden = False
    held = []
    ready = []
    relayed = 0
    for n, event in enumerate(events):
        pos = slab_pos(event)
        slab = wbuf.at[pos[0], pos[1]]
        rcopy(slab, slab, ag_send.at[n], ag_recv.at[n], partner).wait_recv()
        for sent in follow(ring, event):
            send_along(sent, pos)
        cls = class_of(event)
        left_in_class[cls] -= 1
        if left_in_class[cls] == 0:
            if cls[1] < whole:
                x_start(*cls)
                ready.append((cls[1], n))
            else:
                held.append(cls)
        if relayed < whole - 1:
            both = [m for i, m in ready if i == relayed]
            if len(both) == 2 and n >= max(both) + 18:
                x_relay(relayed)
                relayed += 1
        todo.append(pos)
        if n >= min(10, len(events) - 1):
            if not have_hidden:
                hid_local.wait()
                hid_out.wait_recv()
                have_hidden = True
            for _ in range(min(2, len(todo))):
                multiply(todo.pop(0))
    for pos in todo:
        multiply(pos)

    cols = pl.ds(pl.multiple_of(c * 256, 256), 256)
    lx = rcopy(acc.at[128:256], full.at[:, cols], lx_send, lx_recv, partner)
    lx.start()
    full[:, cols] = acc[0:128, :]
    other = full.at[:, pl.ds(pl.multiple_of((1 - c) * 256, 256), 256)]
    rcopy(other, other, lx_send, lx_recv, partner).wait_recv()

    t_logits = full[:, 0:384]
    d_logits = full[:, 384:512]
    t_max = jnp.max(t_logits, axis=1, keepdims=True)
    t_exp = jnp.exp(t_logits - t_max)
    t_sum = jnp.sum(t_exp, axis=1, keepdims=True)
    d_max = jnp.max(d_logits, axis=1, keepdims=True)
    d_sum = jnp.sum(jnp.exp(d_logits - d_max), axis=1, keepdims=True)
    covers = []
    for t in range(4):
        rows = slice(32 * t, 32 * t + 32)
        total = jnp.zeros((32, 128), F32)
        for d in range(nx):
            wanted = list_ref[t, xmod(x + d)]
            piece = jnp.zeros((32, 128), F32)
            for b in range(3):
                keep = jnp.where(wanted == 3 * x + b, 1.0, 0.0).astype(F32)
                piece += keep * t_exp[rows, 128 * b:128 * b + 128]
            if d == 0:
                eown[rows, :] = piece
            else:
                msg[d - 1, rows, :] = piece
            total += piece
        covers.append(jnp.sum(total, axis=1, keepdims=True))
    cover = jnp.concatenate(covers, axis=0)
    lane = lax.broadcasted_iota(jnp.int32, (128, 128), 1)
    stats = jnp.zeros((128, 128), F32)
    for i, value in enumerate((t_max, t_sum, cover, d_max, d_sum)):
        stats = jnp.where(lane == i, value, stats)
    stats_row = stats.T[0:8, :]
    for d in range(1, nx):
        msg[d - 1, 128:136, :] = stats_row

    def sm_copy(d):
        return rcopy(msg.at[d - 1], msgr.at[d - 1], sm_send.at[d - 1], sm_recv.at[d - 1], (xmod(x + d), r))

    for d in range(1, nx):
        sm_copy(d).start()
    for cls in held:
        x_start(*cls)
    for i in range(relayed, whole):
        x_relay(i)
    for d in range(1, nx):
        sm_copy(d).wait_recv()
    stat = [(t_max, t_sum, cover, d_max, d_sum)]
    for d in range(1, nx):
        got = jnp.concatenate([msgr[d - 1, 128:136, :]] * 16, axis=0).T
        stat.append(tuple(got[:, i:i + 1] for i in range(5)))
    all_tmax = functools.reduce(jnp.maximum, [s[0] for s in stat])
    all_dmax = functools.reduce(jnp.maximum, [s[3] for s in stat])
    t_scale = [jnp.exp(s[0] - all_tmax) for s in stat]
    all_tsum = sum(s[1] * a for s, a in zip(stat, t_scale))
    all_dsum = sum(s[4] * jnp.exp(s[3] - all_dmax) for s in stat)
    covered = sum(s[2] * a for s, a in zip(stat, t_scale)) / all_tsum
    target = eown[...] * (t_scale[0] / all_tsum)
    for d in range(1, nx):
        target += msgr[d - 1, 0:128, :] * (t_scale[d] / all_tsum)
    prob = jnp.exp(d_logits - all_dmax) / all_dsum
    lgall[x, 0:128, :] = (covered * prob - target).astype(BF16)

    def lg_copies():
        src = lgall.at[x, 0:128]
        out = [rcopy(src, lgall.at[x, 128:256], lg_send.at[0, 1], lg_recv.at[0, 1], partner)]
        for d in range(1, nx):
            xx = xmod(x + d)
            out.append(rcopy(src, lgall.at[x, 0:128], lg_send.at[d, 0], lg_recv.at[d, 0], (xx, r)))
            out.append(
                rcopy(src, lgall.at[x, 128:256], lg_send.at[d, 1], lg_recv.at[d, 1], (xx, chip * 2 + 1 - c))
            )
        return out

    def lg_wait(d, side):
        group = xmod(x - d)
        slot = lgall.at[group, 128 * side:128 * side + 128]
        rcopy(slot, slot, lg_send.at[d, side], lg_recv.at[d, side], partner).wait_recv()

    for copy in lg_copies():
        copy.start()
    crossed = jnp.sum(target * d_logits, axis=1, keepdims=True)
    crs[...] = jnp.broadcast_to(crossed, (128, 128)).T[0:8, :]

    def cr_copy(d):
        return rcopy(crs, crsr.at[d - 1], cr_send.at[d - 1], cr_recv.at[d - 1], (xmod(x + d), r))

    for d in range(1, nx):
        cr_copy(d).start()

    lg_wait(0, 1)
    lg_t = lgall[x].astype(F32).T.astype(BF16)
    odd = lax.rem(p + q + c, 2)

    def partial(pp, i):
        qq = 2 * i + lax.rem(pp + c, 2)
        lanes = pl.ds(pl.multiple_of(chip_of(pp, qq) * 128, 128), 128)
        return jnp.dot(lg_t, hb[:, lanes], preferred_element_type=F32)

    def rs_copy(d):
        return rcopy(rss.at[d - 1], rsr.at[d - 1], rs_send.at[d - 1], rs_recv.at[d - 1], at(p + d, q))

    for d in sorted(range(1, ring), key=lambda d: -min(d, ring - d)):
        for i in range(half):
            rss[d - 1, i] = partial(mod(p + d), i).astype(BF16)
        rs_copy(d).start()
    for i in range(half):
        rso[i] = partial(p, i)

    loss = covered * (all_dmax + jnp.log(all_dsum))
    loss_row = jnp.broadcast_to(loss, (128, 128)).T[0:8, :] - crs[...]
    for d in range(1, nx):
        cr_copy(d).wait_recv()
        loss_row -= crsr[d - 1]
    loss_ref[...] = loss_row

    for d in range(1, nx):
        for side in (0, 1):
            lg_wait(d, side)

    wide = ring * 128
    piece_wide = part * 128

    def class_y(h, i):
        return mod(y + i - h * (1 + 2 * i))

    def gh_lanes(h, i, xx):
        if i < whole:
            return pl.ds(pl.multiple_of(class_y(h, i) * wide, wide), wide)
        return pl.ds(pl.multiple_of(class_y(h, i) * wide + xx * piece_wide, piece_wide), piece_wide)

    def gh_src(i, side):
        return ghs.at[i, 128 * side:128 * side + 128, 0:wide if i < whole else piece_wide]

    def gh_copies(i):
        lanes = gh_lanes(c, i, x)
        mine = pltpu.make_async_copy(gh_src(i, 0), gh_ref.at[:, lanes], gh_loc.at[i])
        theirs = rcopy(gh_src(i, 1), gh_ref.at[:, lanes], gh_send.at[i], gh_recv.at[i], partner)
        return mine, theirs

    def gx_copies(i):
        out = []
        if nx > 1:
            lanes = gh_lanes(c, i, x)
            for side in (0, 1):
                core = chip * 2 + (c if side == 0 else 1 - c)
                for kind, xx in ((0, xmod(x + 1)), (1, xmod(x - 1))):
                    out.append(
                        rcopy(
                            gh_src(i, side), gh_ref.at[:, lanes], gx_send.at[side, i - whole, kind],
                            gx_recv.at[side, i - whole, kind], (xx, core),
                        )
                    )
        return out

    def gx_arrived(side, i, kind):
        h = c if side == 0 else 1 - c
        xx = {0: xmod(x - 1), 1: xmod(x + 1), 2: xmod(x + 2)}[kind]
        slot = gh_ref.at[:, gh_lanes(h, i, xx)]
        return rcopy(slot, slot, gy_send.at[side, i - whole], gx_recv.at[side, i - whole, kind], (xmod(x + 1), r))

    def gx_relay(side, i):
        kind = (i - whole) % 2
        gx_arrived(side, i, kind).wait_recv()
        h = c if side == 0 else 1 - c
        slot = gh_ref.at[:, gh_lanes(h, i, xmod(x - 1) if kind == 0 else xmod(x + 1))]
        dev = (xmod(x + 1) if kind == 0 else xmod(x - 1), r)
        rcopy(slot, slot, gy_send.at[side, i - whole], gx_recv.at[side, i - whole, 2], dev).start()

    for i in range(whole, half):
        for d in range(nx):
            slot = dq.at[xmod(x - d), i - whole]
            if d == 0:
                @pl.when(c == 1)
                def _():
                    dq_copies(1, i)[0].wait()

                @pl.when(c == 0)
                def _():
                    rcopy(slot, slot, dq_send.at[0, 0, 0], dq_recv.at[0, i - whole], partner).wait_recv()
            else:
                rcopy(slot, slot, dq_send.at[0, 0, 0], dq_recv.at[d, i - whole], partner).wait_recv()

        for s in range(part):
            summed = jnp.zeros((256, 128), F32)
            for g in range(nx):
                piece = lax.dot_general(lgall[g], dq[g, i - whole, s], NT, preferred_element_type=F32)
                summed += piece.astype(BF16).astype(F32)
            ghs[i, :, 128 * s:128 * s + 128] = summed.astype(BF16)
        for copy in (*gx_copies(i), *gh_copies(i)):
            copy.start()

    for i in range(whole):
        if nx > 1:
            for kind in (0, 1, 2):
                if kind == i % 2:
                    continue
                x_arrived(kind, i).wait_recv()

        @pl.when(c == 0)
        def _():
            x_arrived(3, i).wait_recv()

        @pl.when(c == 1)
        def _():
            pltpu.make_async_copy(wbuf.at[:, class_q(1, i), :, 128:256], dall.at[x, i], xg_recv.at[3, i]).wait()

        def width(s, carry):
            summed = jnp.zeros((256, 128), F32)
            for g in range(nx):
                piece = lax.dot_general(lgall[g], dall[g, i, s], NT, preferred_element_type=F32)
                summed += piece.astype(BF16).astype(F32)
            ghs[i, :, pl.ds(pl.multiple_of(s * 128, 128), 128)] = summed.astype(BF16)
            return carry

        lax.fori_loop(0, ring, width, 0)
        for copy in gh_copies(i):
            copy.start()

    if nx == 4:
        for i in range(whole, half):
            for side in (0, 1):
                gx_relay(side, i)

    for d in range(1, ring):
        rs_copy(d).wait_recv()

    def add_up(i, carry):
        total = rso[i]
        for d in range(1, ring):
            total += rsr[d - 1, i].astype(F32)
        fsd[i] = total.T
        return carry

    lax.fori_loop(0, half, add_up, 0)

    def f_copy(i, core):
        d = odd + 2 * i
        qq = mod(q + d)
        j = (qq - lax.rem(p + c, 2)) // 2
        dev = (x, chip_of(p, qq) * 2 + core)
        return rcopy(
            fsd.at[j, 64 * core:64 * core + 64], fin.at[d], f_send.at[i, core], f_recv.at[d], dev
        )

    def f_stays(i, core):
        return jnp.logical_and(odd + 2 * i == 0, core == c)

    for i in range(half):
        for core in (0, 1):
            stays = f_stays(i, core)

            @pl.when(jnp.logical_not(stays))
            def _():
                f_copy(i, core).start()

            @pl.when(stays)
            def _():
                j = (q - lax.rem(p + c, 2)) // 2
                fin[0] = fsd[j, 64 * core:64 * core + 64, :]

    home = lax.rem(y + z + c, 2) == 0
    grad = jnp.zeros((64, 128), F32)
    for d in range(ring):
        slot = fin.at[d]
        arrival = rcopy(slot, slot, f_send.at[0, 0], f_recv.at[d], partner)
        if d == 0:
            pl.when(jnp.logical_not(home))(arrival.wait_recv)
        else:
            arrival.wait_recv()
        grad += fin[d]
    gd_ref[...] = grad

    for i in range(half):
        mine, theirs = gh_copies(i)
        mine.wait()
        theirs.wait_send()
    for i in range(half):
        slot = gh_ref.at[:, gh_lanes(1 - c, i, x)]
        rcopy(slot, slot, gh_send.at[i], gh_recv.at[i], partner).wait_recv()
    if nx == 4:
        for i in range(whole, half):
            for side in (0, 1):
                for kind in (0, 1, 2):
                    if kind != (i - whole) % 2:
                        gx_arrived(side, i, kind).wait_recv()
                gx_arrived(side, i, 0).wait_send()
            for copy in gx_copies(i):
                copy.wait_send()
    for i in range(half):
        for core in (0, 1):
            @pl.when(jnp.logical_not(f_stays(i, core)))
            def _():
                f_copy(i, core).wait_send()
    for d in range(1, ring):
        rs_copy(d).wait_send()
    for d in range(1, nx):
        cr_copy(d).wait_send()
        sm_copy(d).wait_send()
    for copy in lg_copies():
        copy.wait_send()
    lx.wait_send()
    hid_out.wait_send()

    @pl.when(c == 0)
    def _():
        to_b1.wait_send()
        to_b2.wait_send()

    @pl.when(c == 1)
    def _():
        to_a.wait_send()
        for h in (0, 1):
            for i in range(whole):
                for n, copy in enumerate(x_copies(h, i)):
                    if nx > 1 and n < 2 or h == 0:
                        copy.wait_send()
            for i in range(whole, half):
                for d, copy in enumerate(dq_copies(h, i)):
                    if d > 0 or h == 0:
                        copy.wait_send()

    if nx == 4:
        for i in range(whole):
            x_arrived(0, i).wait_send()
    for n, event in enumerate(events):
        slab = wbuf.at[0, 0]
        rcopy(slab, slab, ag_send.at[n], ag_recv.at[n], partner).wait_send()


def deliver(tiles, loss_in, gh_in, gd_in, loss_out, gh_out, gd_out, wide_loss, loss_buf, gh_buf, gd_buf, come, go):
    rows = gh_in.shape[0] // CHUNKS
    chunks = [slice(rows * n, rows * n + rows) for n in range(CHUNKS)]
    take_loss = pltpu.make_async_copy(loss_in, wide_loss, come.at[CHUNKS])
    take_gd = pltpu.make_async_copy(gd_in, gd_buf, come.at[CHUNKS + 1])
    put_loss = pltpu.make_async_copy(loss_buf, loss_out, go.at[CHUNKS])
    put_gd = pltpu.make_async_copy(gd_buf, gd_out, go.at[CHUNKS + 1])
    take = [pltpu.make_async_copy(gh_in.at[k], gh_buf.at[k], come.at[n]) for n, k in enumerate(chunks)]
    put = [pltpu.make_async_copy(gh_buf.at[k], gh_out.at[k], go.at[n]) for n, k in enumerate(chunks)]
    for copy in (take_loss, take_gd, *take):
        copy.start()
    take_loss.wait()
    lanes = loss_buf.shape[1]
    for t in range(tiles):
        loss_buf[t:t + 1, :] = wide_loss[0:1, lanes * t:lanes * t + lanes]
    put_loss.start()
    take_gd.wait()
    put_gd.start()
    for taken, given in zip(take, put):
        taken.wait()
        given.start()
    for copy in (put_loss, put_gd, *put):
        copy.wait()


def per_device(nx, ring, hidden, teacher_weight, draft_weight, draft_list):
    tiles, tile_rows, width = hidden.shape
    rows = tiles * tile_rows
    half = ring // 2
    whole = half // 2
    parts = half - whole
    dma = pltpu.SemaphoreType.DMA
    more = max(nx - 1, 1)
    scratch = [
        pltpu.VMEM((ring, ring, 128, 256), BF16),
        pltpu.VMEM((2 * rows, width), BF16),
        pltpu.VMEM((2 * rows, 256), F32),
        pltpu.VMEM((rows, 512), F32),
        pltpu.VMEM((nx, max(whole, 1), ring, 128, 128), BF16),
        pltpu.VMEM((nx, half - whole, ring // nx, 128, 128), BF16),
        pltpu.VMEM((more, rows + 8, 128), F32),
        pltpu.VMEM((more, rows + 8, 128), F32),
        pltpu.VMEM((rows, 128), F32),
        pltpu.VMEM((nx, 2 * rows, 128), BF16),
        pltpu.VMEM((8, 128), F32),
        pltpu.VMEM((more, 8, 128), F32),
        pltpu.VMEM((ring - 1, half, 128, 128), BF16),
        pltpu.VMEM((ring - 1, half, 128, 128), BF16),
        pltpu.VMEM((half, 128, 128), F32),
        pltpu.VMEM((half, 128, 128), F32),
        pltpu.VMEM((ring, 64, 128), F32),
        pltpu.VMEM((half, 2 * rows, ring * 128), BF16),
        dma((6,)), dma((3,)), dma((ring * ring,)), dma((ring * ring,)),
        dma((2, half, 3)), dma((4, half)), dma((half,)), dma((2, parts, nx)), dma((nx, parts)),
        dma(()), dma(()), dma((more,)), dma((more,)),
        dma((nx, 2)), dma((nx, 2)), dma((more,)), dma((more,)),
        dma((ring - 1,)), dma((ring - 1,)), dma((half, 2)), dma((ring,)),
        dma((half,)), dma((half,)), dma((half,)),
        dma((2, parts, 2)), dma((2, parts, 3)), dma((2, parts)),
    ]
    hbm = pl.BlockSpec(memory_space=pl.ANY)
    vmem = pl.BlockSpec(memory_space=pltpu.VMEM)
    loss, grad_hidden, grad_draft = pl.pallas_call(
        functools.partial(kernel, nx, ring),
        out_shape=(
            jax.ShapeDtypeStruct((8, 128), F32),
            jax.ShapeDtypeStruct((rows, width), BF16),
            jax.ShapeDtypeStruct((64, 128), F32),
        ),
        in_specs=[pl.BlockSpec(memory_space=pltpu.SMEM), hbm, hbm, hbm],
        out_specs=(vmem, hbm, vmem),
        scratch_shapes=scratch,
        compiler_params=pltpu.CompilerParams(
            collective_id=0, has_side_effects=True, vmem_limit_bytes=60 * 1024 * 1024
        ),
        name="distill",
    )(draft_list, hidden.reshape(rows, width), teacher_weight, draft_weight)
    loss, grad_hidden, grad_draft = pl.pallas_call(
        functools.partial(deliver, tiles),
        out_shape=(
            jax.ShapeDtypeStruct((tiles, tile_rows), F32),
            jax.ShapeDtypeStruct((rows, width), BF16),
            jax.ShapeDtypeStruct((64, 128), F32),
        ),
        in_specs=[hbm, hbm, hbm],
        out_specs=(hbm, hbm, hbm),
        scratch_shapes=[
            pltpu.VMEM((8, 128), F32), pltpu.VMEM((tiles, tile_rows), F32), pltpu.VMEM((rows, width), BF16),
            pltpu.VMEM((64, 128), F32), dma((CHUNKS + 2,)), dma((CHUNKS + 2,)),
        ],
        compiler_params=pltpu.CompilerParams(vmem_limit_bytes=60 * 1024 * 1024),
        name="deliver",
    )(loss, grad_hidden, grad_draft)
    return loss, grad_hidden.reshape(hidden.shape), grad_draft


def solution(mesh):
    nx, devices = mesh.shape["vocab"], mesh.shape["rows"]
    ring = int(round((devices // 2) ** 0.5))
    in_specs = (P(None, "rows", None), P("rows", "vocab"), P("rows", "vocab"), P())
    out_specs = (P(None, "rows"), P(None, "rows", None), P("rows", "vocab"))
    return jax.shard_map(
        functools.partial(per_device, nx, ring), mesh=mesh, in_specs=in_specs, out_specs=out_specs, check_vma=False
    )
```

```python
import functools
import heapq

import jax
import jax.numpy as jnp
from jax import lax
from jax.experimental import pallas as pl
from jax.experimental.pallas import tpu as pltpu
from jax.sharding import PartitionSpec as P

CHUNKS = 8
F32 = jnp.float32
BF16 = jnp.bfloat16
MESH = pl.DeviceIdType.MESH
NT = (((1,), (1,)), ((), ()))


def offset_of(k):
    return 0 if k == 0 else (-(k + 1) // 2 if k % 2 else k // 2)


def reach(ring, kind, k):
    half = ring // 2
    if kind == "P" or k % 2 == 0:
        return {"R": half, "L": half - 1}
    return {"R": half - 1, "L": half}


def follow(ring, event):
    kind, k, way, dist = event
    sends = []
    if kind == "P":
        if way is None:
            sends += [("P", 0, w, 1) for w in "RL" if reach(ring, "P", 0)[w] >= 1]
            first = 0
        else:
            if dist < reach(ring, "P", 0)[way]:
                sends.append(("P", 0, way, dist + 1))
            first = 2 * dist - 1 if way == "R" else 2 * dist
        sends += [("Q", first, w, 1) for w in "RL" if reach(ring, "Q", first)[w] >= 1]
    elif dist < reach(ring, "Q", k)[way]:
        sends.append(("Q", k, way, dist + 1))
    return sends


def event_order(ring, slab_us=0.7, hop_us=1.7, step_us=0.2):
    free = {"R": 0.0, "L": 0.0}
    arrivals, order, now, count = [], [], 0.0, 0
    pending = [("P", 0, None, 0)]
    while True:
        for event in pending:
            for sent in follow(ring, event):
                way = sent[2]
                free[way] = max(free[way], now) + slab_us
                count += 1
                heapq.heappush(arrivals, (free[way] + hop_us, count, sent))
        if not arrivals:
            return order
        when, _, event = heapq.heappop(arrivals)
        now = max(now + step_us, when)
        order.append(event)
        pending = [event]


def kernel(
    nx, ring, list_ref, hid_ref, tw_ref, dw_ref, loss_ref, gh_ref, gd_ref,
    wbuf, hb, acc, full, dall, dq, msg, msgr, stm, stmr, eown, lgall, crs, crsr, rss, rsr, rso, fsd, fin, ghs,
    init_sem, hid_sem, ag_send, ag_recv, xg_send, xg_recv, xr_send, dq_send, dq_recv, lx_send, lx_recv, sm_send, sm_recv, st_send, st_recv,
    lg_send, lg_recv, cr_send, cr_recv, rs_send, rs_recv, f_send, f_recv, gh_send, gh_recv, gh_loc,
    gx_send, gx_recv, gy_send,
):
    x = lax.axis_index("vocab")
    r = lax.axis_index("rows")
    c = lax.rem(r, 2)
    chip = r // 2
    y, z = chip // ring, lax.rem(chip, ring)
    p = y + c * (z - y)
    q = z + c * (y - z)
    half = ring // 2
    whole = half // 2
    part = ring // nx

    def mod(v):
        return lax.rem(v + 2 * ring, ring)

    def xmod(v):
        return lax.rem(v + nx, nx)

    def chip_of(pp, qq):
        straight, turned = pp * ring + qq, qq * ring + pp
        return straight + c * (turned - straight)

    def at(pp, qq):
        return (x, chip_of(mod(pp), mod(qq)) * 2 + c)

    partner = (x, chip * 2 + 1 - c)

    def rcopy(src, dst, ssem, rsem, dev):
        return pltpu.make_async_remote_copy(
            src_ref=src, dst_ref=dst, send_sem=ssem, recv_sem=rsem, device_id=dev, device_id_type=MESH
        )

    hid_local = pltpu.make_async_copy(hid_ref, hb.at[0:128], hid_sem.at[0])
    own = wbuf.at[p, q]
    loc_a0 = pltpu.make_async_copy(tw_ref.at[:, 0:256], own.at[0:64, :], init_sem.at[0])
    loc_b1 = pltpu.make_async_copy(tw_ref.at[:, 256:384], own.at[64:128, 0:128], init_sem.at[0])
    loc_b2 = pltpu.make_async_copy(dw_ref, own.at[64:128, 128:256], init_sem.at[1])

    @pl.when(c == 0)
    def _():
        loc_a0.start()

    @pl.when(c == 1)
    def _():
        loc_b1.start()
        loc_b2.start()

    hid_local.start()

    barrier = pltpu.get_barrier_semaphore()
    greeted = 0
    for d in range(1, ring):
        for core in (0, 1):
            for dev in ((mod(y + d) * ring + z), (y * ring + mod(z + d))):
                pl.semaphore_signal(barrier, inc=1, device_id=(x, dev * 2 + core), device_id_type=MESH)
                greeted += 1
    for d in range(1, nx):
        for core in (0, 1):
            pl.semaphore_signal(barrier, inc=1, device_id=(xmod(x + d), chip * 2 + core), device_id_type=MESH)
            greeted += 1
    pl.semaphore_signal(barrier, inc=1, device_id=partner, device_id_type=MESH)
    pl.semaphore_wait(barrier, greeted + 1)

    there = wbuf.at[q, p]
    to_b1 = rcopy(tw_ref.at[:, 256:384], there.at[0:64, 0:128], init_sem.at[2], init_sem.at[4], partner)
    to_b2 = rcopy(dw_ref, there.at[0:64, 128:256], init_sem.at[3], init_sem.at[5], partner)
    to_a = rcopy(tw_ref.at[:, 0:256], there.at[64:128, :], init_sem.at[2], init_sem.at[4], partner)
    from_a1 = rcopy(tw_ref.at[:, 256:384], own.at[0:64, 0:128], init_sem.at[2], init_sem.at[4], partner)
    from_a2 = rcopy(dw_ref, own.at[0:64, 128:256], init_sem.at[3], init_sem.at[5], partner)
    from_b = rcopy(tw_ref.at[:, 0:256], own.at[64:128, :], init_sem.at[2], init_sem.at[4], partner)

    @pl.when(c == 0)
    def _():
        to_b1.start()
        to_b2.start()

    @pl.when(c == 1)
    def _():
        to_a.start()

    hid_out = rcopy(hid_ref, hb.at[128:256], hid_sem.at[1], hid_sem.at[2], partner)
    hid_out.start()

    @pl.when(c == 0)
    def _():
        loc_a0.wait()
        from_b.wait_recv()

    @pl.when(c == 1)
    def _():
        loc_b1.wait()
        loc_b2.wait()
        from_a1.wait_recv()
        from_a2.wait_recv()

    events = event_order(ring)
    number = {event: i for i, event in enumerate(events)}

    def slab_pos(event):
        kind, k, way, dist = event
        step = -dist if way == "R" else dist
        if kind == "P":
            return mod(p + step), q
        return mod(p + offset_of(k)), mod(q + step)

    def send_along(sent, pos):
        kind, _, way, _ = sent
        step = 1 if way == "R" else -1
        dev = at(p + step, q) if kind == "P" else at(p, q + step)
        i = number[sent]
        slab = wbuf.at[pos[0], pos[1]]
        rcopy(slab, slab, ag_send.at[i], ag_recv.at[i], dev).start()

    def multiply(pos):
        pp, qq = pos
        lanes = pl.ds(pl.multiple_of(chip_of(pp, qq) * 128, 128), 128)
        acc[...] += jnp.dot(hb[:, lanes], wbuf[pp, qq], preferred_element_type=F32)

    def class_of(event):
        kind, k, way, dist = event
        if kind == "P":
            return (0, 0)
        if dist == half:
            return (1, half - 1)
        return (0, dist) if way == "L" else (1, dist - 1)

    left_in_class = {}
    for event in events:
        left_in_class[class_of(event)] = left_in_class.get(class_of(event), 0) + 1

    def class_q(h, i):
        return mod(q + i) if h == 0 else mod(q - 1 - i)

    def x_copies(h, i):
        src = wbuf.at[:, class_q(h, i), :, 128:256]
        dst = dall.at[x, i]
        out = []
        if nx > 1:
            out.append(rcopy(src, dst, xg_send.at[h, i, 0], xg_recv.at[0, i], (xmod(x + 1), chip * 2 + h)))
            out.append(rcopy(src, dst, xg_send.at[h, i, 1], xg_recv.at[1, i], (xmod(x - 1), chip * 2 + h)))
        if h == 0:
            out.append(rcopy(src, dst, xg_send.at[h, i, 2], xg_recv.at[3, i], (x, chip * 2)))
        else:
            out.append(pltpu.make_async_copy(src, dst, xg_recv.at[3, i]))
        return out

    def dq_copies(h, i):
        out = []
        for d in range(nx):
            xx = xmod(x + d)
            src = wbuf.at[pl.ds(part * xx, part), class_q(h, i), :, 128:256]
            dst = dq.at[x, i - whole]
            if d == 0 and h == 1:
                out.append(pltpu.make_async_copy(src, dst, dq_recv.at[0, i - whole]))
            else:
                dev = (xx, chip * 2 + h)
                out.append(rcopy(src, dst, dq_send.at[h, i - whole, d], dq_recv.at[d, i - whole], dev))
        return out

    def x_start(h, i):
        @pl.when(c == 1)
        def _():
            for copy in x_copies(h, i) if i < whole else dq_copies(h, i):
                copy.start()

    def x_arrived(kind, i):
        group = {0: xmod(x - 1), 1: xmod(x + 1), 2: xmod(x + 2), 3: x}[kind]
        slot = dall.at[group, i]
        return rcopy(slot, slot, xr_send.at[i], xg_recv.at[kind, i], (xmod(x + 1), r))

    def x_relay(i):
        if nx == 4:
            kind = i % 2
            x_arrived(kind, i).wait_recv()
            group = xmod(x - 1) if kind == 0 else xmod(x + 1)
            dev = (xmod(x + 1), r) if kind == 0 else (xmod(x - 1), r)
            slot = dall.at[group, i]
            rcopy(slot, slot, xr_send.at[i], xg_recv.at[2, i], dev).start()

    for sent in follow(ring, ("P", 0, None, 0)):
        send_along(sent, (p, q))
    acc[...] = jnp.zeros_like(acc)

    todo = [(p, q)]
    have_hidden = False
    held = []
    relay_at = {}
    for n, event in enumerate(events):
        pos = slab_pos(event)
        slab = wbuf.at[pos[0], pos[1]]
        rcopy(slab, slab, ag_send.at[n], ag_recv.at[n], partner).wait_recv()
        for sent in follow(ring, event):
            send_along(sent, pos)
        cls = class_of(event)
        left_in_class[cls] -= 1
        if left_in_class[cls] == 0:
            if cls[1] < whole:
                x_start(*cls)
                relay_at.setdefault(n + 16, []).append(cls)
            else:
                held.append(cls)
        for h, i in relay_at.pop(n, ()):
            pl.when(c == h)(functools.partial(x_relay, i))
        todo.append(pos)
        if n >= min(10, len(events) - 1):
            if not have_hidden:
                hid_local.wait()
                hid_out.wait_recv()
                have_hidden = True
            for _ in range(min(2, len(todo))):
                multiply(todo.pop(0))
    for pos in todo:
        multiply(pos)

    cols = pl.ds(pl.multiple_of(c * 256, 256), 256)
    lx = rcopy(acc.at[128:256], full.at[:, cols], lx_send, lx_recv, partner)
    lx.start()
    full[:, cols] = acc[0:128, :]
    other = full.at[:, pl.ds(pl.multiple_of((1 - c) * 256, 256), 256)]
    rcopy(other, other, lx_send, lx_recv, partner).wait_recv()

    t_logits = full[:, 0:384]
    d_logits = full[:, 384:512]
    t_max = jnp.max(t_logits, axis=1, keepdims=True)
    t_exp = jnp.exp(t_logits - t_max)
    t_sum = jnp.sum(t_exp, axis=1, keepdims=True)

    def sm_copy(d):
        return rcopy(msg.at[d - 1], msgr.at[d - 1], sm_send.at[d - 1], sm_recv.at[d - 1], (xmod(x + d), r))

    def st_copy(d):
        return rcopy(stm, stmr.at[d - 1], st_send.at[d - 1], st_recv.at[d - 1], (xmod(x + d), r))

    totals = [jnp.zeros((32, 128), F32) for _ in range(4)]
    for d in sorted(range(nx), key=lambda d: -min(d, nx - d)):
        for t in range(4):
            rows = slice(32 * t, 32 * t + 32)
            wanted = list_ref[t, xmod(x + d)]
            piece = jnp.zeros((32, 128), F32)
            for b in range(3):
                keep = jnp.where(wanted == 3 * x + b, 1.0, 0.0).astype(F32)
                piece += keep * t_exp[rows, 128 * b:128 * b + 128]
            if d == 0:
                eown[rows, :] = piece
            else:
                msg[d - 1, rows, :] = piece.astype(BF16)
            totals[t] += piece
        if d > 0:
            sm_copy(d).start()
    cover = jnp.concatenate([jnp.sum(total, axis=1, keepdims=True) for total in totals], axis=0)
    d_max = jnp.max(d_logits, axis=1, keepdims=True)
    d_sum = jnp.sum(jnp.exp(d_logits - d_max), axis=1, keepdims=True)
    lane = lax.broadcasted_iota(jnp.int32, (128, 128), 1)
    stats = jnp.zeros((128, 128), F32)
    for i, value in enumerate((t_max, t_sum, cover, d_max, d_sum)):
        stats = jnp.where(lane == i, value, stats)
    stm[...] = stats.T[0:8, :]
    for d in range(1, nx):
        st_copy(d).start()
    for cls in held:
        x_start(*cls)
    for n in sorted(relay_at):
        for h, i in relay_at[n]:
            pl.when(c == h)(functools.partial(x_relay, i))
    for d in range(1, nx):
        st_copy(d).wait_recv()
    stat = [(t_max, t_sum, cover, d_max, d_sum)]
    for d in range(1, nx):
        got = jnp.concatenate([stmr[d - 1]] * 16, axis=0).T
        stat.append(tuple(got[:, i:i + 1] for i in range(5)))
    all_tmax = functools.reduce(jnp.maximum, [s[0] for s in stat])
    all_dmax = functools.reduce(jnp.maximum, [s[3] for s in stat])
    t_scale = [jnp.exp(s[0] - all_tmax) for s in stat]
    all_tsum = sum(s[1] * a for s, a in zip(stat, t_scale))
    all_dsum = sum(s[4] * jnp.exp(s[3] - all_dmax) for s in stat)
    covered = sum(s[2] * a for s, a in zip(stat, t_scale)) / all_tsum
    target = eown[...] * (t_scale[0] / all_tsum)
    prob = jnp.exp(d_logits - all_dmax) / all_dsum
    for d in range(1, nx):
        sm_copy(d).wait_recv()
        target += msgr[d - 1].astype(F32) * (t_scale[d] / all_tsum)
    lgall[x, 0:128, :] = (covered * prob - target).astype(BF16)

    def lg_copies():
        src = lgall.at[x, 0:128]
        out = [rcopy(src, lgall.at[x, 128:256], lg_send.at[0, 1], lg_recv.at[0, 1], partner)]
        for d in range(1, nx):
            xx = xmod(x + d)
            out.append(rcopy(src, lgall.at[x, 0:128], lg_send.at[d, 0], lg_recv.at[d, 0], (xx, r)))
            out.append(
                rcopy(src, lgall.at[x, 128:256], lg_send.at[d, 1], lg_recv.at[d, 1], (xx, chip * 2 + 1 - c))
            )
        return out

    def lg_wait(d, side):
        group = xmod(x - d)
        slot = lgall.at[group, 128 * side:128 * side + 128]
        rcopy(slot, slot, lg_send.at[d, side], lg_recv.at[d, side], partner).wait_recv()

    for copy in lg_copies():
        copy.start()
    crossed = jnp.sum(target * d_logits, axis=1, keepdims=True)
    crs[...] = jnp.broadcast_to(crossed, (128, 128)).T[0:8, :]

    def cr_copy(d):
        return rcopy(crs, crsr.at[d - 1], cr_send.at[d - 1], cr_recv.at[d - 1], (xmod(x + d), r))

    for d in range(1, nx):
        cr_copy(d).start()

    lg_wait(0, 1)
    lg_t = lgall[x].astype(F32).T.astype(BF16)
    odd = lax.rem(p + q + c, 2)

    def partial(pp, i):
        qq = 2 * i + lax.rem(pp + c, 2)
        lanes = pl.ds(pl.multiple_of(chip_of(pp, qq) * 128, 128), 128)
        return jnp.dot(lg_t, hb[:, lanes], preferred_element_type=F32)

    def rs_copy(d):
        return rcopy(rss.at[d - 1], rsr.at[d - 1], rs_send.at[d - 1], rs_recv.at[d - 1], at(p + d, q))

    for d in sorted(range(1, ring), key=lambda d: -min(d, ring - d)):
        for i in range(half):
            rss[d - 1, i] = partial(mod(p + d), i).astype(BF16)
        rs_copy(d).start()
    for i in range(half):
        rso[i] = partial(p, i)

    loss = covered * (all_dmax + jnp.log(all_dsum))
    loss_row = jnp.broadcast_to(loss, (128, 128)).T[0:8, :] - crs[...]
    for d in range(1, nx):
        cr_copy(d).wait_recv()
        loss_row -= crsr[d - 1]
    loss_ref[...] = loss_row

    for d in range(1, nx):
        for side in (0, 1):
            lg_wait(d, side)

    wide = ring * 128
    piece_wide = part * 128

    def class_y(h, i):
        return mod(y + i - h * (1 + 2 * i))

    def gh_lanes(h, i, xx):
        if i < whole:
            return pl.ds(pl.multiple_of(class_y(h, i) * wide, wide), wide)
        return pl.ds(pl.multiple_of(class_y(h, i) * wide + xx * piece_wide, piece_wide), piece_wide)

    def gh_src(i, side):
        return ghs.at[i, 128 * side:128 * side + 128, 0:wide if i < whole else piece_wide]

    def gh_copies(i):
        lanes = gh_lanes(c, i, x)
        mine = pltpu.make_async_copy(gh_src(i, 0), gh_ref.at[:, lanes], gh_loc.at[i])
        theirs = rcopy(gh_src(i, 1), gh_ref.at[:, lanes], gh_send.at[i], gh_recv.at[i], partner)
        return mine, theirs

    def gx_copies(i):
        out = []
        if nx > 1:
            lanes = gh_lanes(c, i, x)
            for side in (0, 1):
                core = chip * 2 + (c if side == 0 else 1 - c)
                for kind, xx in ((0, xmod(x + 1)), (1, xmod(x - 1))):
                    out.append(
                        rcopy(
                            gh_src(i, side), gh_ref.at[:, lanes], gx_send.at[side, i - whole, kind],
                            gx_recv.at[side, i - whole, kind], (xx, core),
                        )
                    )
        return out

    def gx_arrived(side, i, kind):
        h = c if side == 0 else 1 - c
        xx = {0: xmod(x - 1), 1: xmod(x + 1), 2: xmod(x + 2)}[kind]
        slot = gh_ref.at[:, gh_lanes(h, i, xx)]
        return rcopy(slot, slot, gy_send.at[side, i - whole], gx_recv.at[side, i - whole, kind], (xmod(x + 1), r))

    def gx_relay(side, i):
        kind = (i - whole) % 2
        gx_arrived(side, i, kind).wait_recv()
        h = c if side == 0 else 1 - c
        slot = gh_ref.at[:, gh_lanes(h, i, xmod(x - 1) if kind == 0 else xmod(x + 1))]
        dev = (xmod(x + 1) if kind == 0 else xmod(x - 1), r)
        rcopy(slot, slot, gy_send.at[side, i - whole], gx_recv.at[side, i - whole, 2], dev).start()

    for i in range(whole, half):
        for d in range(nx):
            slot = dq.at[xmod(x - d), i - whole]
            if d == 0:
                @pl.when(c == 1)
                def _():
                    dq_copies(1, i)[0].wait()

                @pl.when(c == 0)
                def _():
                    rcopy(slot, slot, dq_send.at[0, 0, 0], dq_recv.at[0, i - whole], partner).wait_recv()
            else:
                rcopy(slot, slot, dq_send.at[0, 0, 0], dq_recv.at[d, i - whole], partner).wait_recv()

        for s in range(part):
            summed = jnp.zeros((256, 128), F32)
            for g in range(nx):
                piece = lax.dot_general(lgall[g], dq[g, i - whole, s], NT, preferred_element_type=F32)
                summed += piece.astype(BF16).astype(F32)
            ghs[i, :, 128 * s:128 * s + 128] = summed.astype(BF16)
        for copy in (*gx_copies(i), *gh_copies(i)):
            copy.start()

    for i in range(whole):
        if nx > 1:
            for kind in (0, 1, 2):
                if kind == i % 2:
                    continue
                x_arrived(kind, i).wait_recv()

        @pl.when(c == 0)
        def _():
            x_arrived(3, i).wait_recv()

        @pl.when(c == 1)
        def _():
            pltpu.make_async_copy(wbuf.at[:, class_q(1, i), :, 128:256], dall.at[x, i], xg_recv.at[3, i]).wait()

        def width(s, carry):
            summed = jnp.zeros((256, 128), F32)
            for g in range(nx):
                piece = lax.dot_general(lgall[g], dall[g, i, s], NT, preferred_element_type=F32)
                summed += piece.astype(BF16).astype(F32)
            ghs[i, :, pl.ds(pl.multiple_of(s * 128, 128), 128)] = summed.astype(BF16)
            return carry

        lax.fori_loop(0, ring, width, 0)
        for copy in gh_copies(i):
            copy.start()

    if nx == 4:
        for i in range(whole, half):
            for side in (0, 1):
                gx_relay(side, i)

    for d in range(1, ring):
        rs_copy(d).wait_recv()

    def add_up(i, carry):
        total = rso[i]
        for d in range(1, ring):
            total += rsr[d - 1, i].astype(F32)
        fsd[i] = total.T.astype(BF16)
        return carry

    lax.fori_loop(0, half, add_up, 0)

    def f_copy(i, core):
        d = odd + 2 * i
        qq = mod(q + d)
        j = (qq - lax.rem(p + c, 2)) // 2
        dev = (x, chip_of(p, qq) * 2 + core)
        return rcopy(
            fsd.at[j, 64 * core:64 * core + 64], fin.at[d], f_send.at[i, core], f_recv.at[d], dev
        )

    def f_stays(i, core):
        return jnp.logical_and(odd + 2 * i == 0, core == c)

    for i in range(half):
        for core in (0, 1):
            stays = f_stays(i, core)

            @pl.when(jnp.logical_not(stays))
            def _():
                f_copy(i, core).start()

            @pl.when(stays)
            def _():
                j = (q - lax.rem(p + c, 2)) // 2
                fin[0] = fsd[j, 64 * core:64 * core + 64, :]

    home = lax.rem(y + z + c, 2) == 0
    grad = jnp.zeros((64, 128), F32)
    for d in range(ring):
        slot = fin.at[d]
        arrival = rcopy(slot, slot, f_send.at[0, 0], f_recv.at[d], partner)
        if d == 0:
            pl.when(jnp.logical_not(home))(arrival.wait_recv)
        else:
            arrival.wait_recv()
        grad += fin[d].astype(F32)
    gd_ref[...] = grad

    for i in range(half):
        mine, theirs = gh_copies(i)
        mine.wait()
        theirs.wait_send()
    for i in range(half):
        slot = gh_ref.at[:, gh_lanes(1 - c, i, x)]
        rcopy(slot, slot, gh_send.at[i], gh_recv.at[i], partner).wait_recv()
    if nx == 4:
        for i in range(whole, half):
            for side in (0, 1):
                for kind in (0, 1, 2):
                    if kind != (i - whole) % 2:
                        gx_arrived(side, i, kind).wait_recv()
                gx_arrived(side, i, 0).wait_send()
            for copy in gx_copies(i):
                copy.wait_send()
    for i in range(half):
        for core in (0, 1):
            @pl.when(jnp.logical_not(f_stays(i, core)))
            def _():
                f_copy(i, core).wait_send()
    for d in range(1, ring):
        rs_copy(d).wait_send()
    for d in range(1, nx):
        cr_copy(d).wait_send()
        sm_copy(d).wait_send()
        st_copy(d).wait_send()
    for copy in lg_copies():
        copy.wait_send()
    lx.wait_send()
    hid_out.wait_send()

    @pl.when(c == 0)
    def _():
        to_b1.wait_send()
        to_b2.wait_send()

    @pl.when(c == 1)
    def _():
        to_a.wait_send()
        for h in (0, 1):
            for i in range(whole):
                for n, copy in enumerate(x_copies(h, i)):
                    if nx > 1 and n < 2 or h == 0:
                        copy.wait_send()
            for i in range(whole, half):
                for d, copy in enumerate(dq_copies(h, i)):
                    if d > 0 or h == 0:
                        copy.wait_send()

    if nx == 4:
        for i in range(whole):
            x_arrived(0, i).wait_send()
    for n, event in enumerate(events):
        slab = wbuf.at[0, 0]
        rcopy(slab, slab, ag_send.at[n], ag_recv.at[n], partner).wait_send()


def deliver(tiles, loss_in, gh_in, gd_in, loss_out, gh_out, gd_out, wide_loss, loss_buf, gh_buf, gd_buf, come, go):
    rows = gh_in.shape[0] // CHUNKS
    chunks = [slice(rows * n, rows * n + rows) for n in range(CHUNKS)]
    take_loss = pltpu.make_async_copy(loss_in, wide_loss, come.at[CHUNKS])
    take_gd = pltpu.make_async_copy(gd_in, gd_buf, come.at[CHUNKS + 1])
    put_loss = pltpu.make_async_copy(loss_buf, loss_out, go.at[CHUNKS])
    put_gd = pltpu.make_async_copy(gd_buf, gd_out, go.at[CHUNKS + 1])
    take = [pltpu.make_async_copy(gh_in.at[k], gh_buf.at[k], come.at[n]) for n, k in enumerate(chunks)]
    put = [pltpu.make_async_copy(gh_buf.at[k], gh_out.at[k], go.at[n]) for n, k in enumerate(chunks)]
    for copy in (take_loss, take_gd, *take):
        copy.start()
    take_loss.wait()
    lanes = loss_buf.shape[1]
    for t in range(tiles):
        loss_buf[t:t + 1, :] = wide_loss[0:1, lanes * t:lanes * t + lanes]
    put_loss.start()
    take_gd.wait()
    put_gd.start()
    for taken, given in zip(take, put):
        taken.wait()
        given.start()
    for copy in (put_loss, put_gd, *put):
        copy.wait()


def per_device(nx, ring, hidden, teacher_weight, draft_weight, draft_list):
    tiles, tile_rows, width = hidden.shape
    rows = tiles * tile_rows
    half = ring // 2
    whole = half // 2
    parts = half - whole
    dma = pltpu.SemaphoreType.DMA
    more = max(nx - 1, 1)
    scratch = [
        pltpu.VMEM((ring, ring, 128, 256), BF16),
        pltpu.VMEM((2 * rows, width), BF16),
        pltpu.VMEM((2 * rows, 256), F32),
        pltpu.VMEM((rows, 512), F32),
        pltpu.VMEM((nx, max(whole, 1), ring, 128, 128), BF16),
        pltpu.VMEM((nx, half - whole, ring // nx, 128, 128), BF16),
        pltpu.VMEM((more, rows, 128), BF16),
        pltpu.VMEM((more, rows, 128), BF16),
        pltpu.VMEM((8, 128), F32),
        pltpu.VMEM((more, 8, 128), F32),
        pltpu.VMEM((rows, 128), F32),
        pltpu.VMEM((nx, 2 * rows, 128), BF16),
        pltpu.VMEM((8, 128), F32),
        pltpu.VMEM((more, 8, 128), F32),
        pltpu.VMEM((ring - 1, half, 128, 128), BF16),
        pltpu.VMEM((ring - 1, half, 128, 128), BF16),
        pltpu.VMEM((half, 128, 128), F32),
        pltpu.VMEM((half, 128, 128), BF16),
        pltpu.VMEM((ring, 64, 128), BF16),
        pltpu.VMEM((half, 2 * rows, ring * 128), BF16),
        dma((6,)), dma((3,)), dma((ring * ring,)), dma((ring * ring,)),
        dma((2, half, 3)), dma((4, half)), dma((half,)), dma((2, parts, nx)), dma((nx, parts)),
        dma(()), dma(()), dma((more,)), dma((more,)), dma((more,)), dma((more,)),
        dma((nx, 2)), dma((nx, 2)), dma((more,)), dma((more,)),
        dma((ring - 1,)), dma((ring - 1,)), dma((half, 2)), dma((ring,)),
        dma((half,)), dma((half,)), dma((half,)),
        dma((2, parts, 2)), dma((2, parts, 3)), dma((2, parts)),
    ]
    hbm = pl.BlockSpec(memory_space=pl.ANY)
    vmem = pl.BlockSpec(memory_space=pltpu.VMEM)
    loss, grad_hidden, grad_draft = pl.pallas_call(
        functools.partial(kernel, nx, ring),
        out_shape=(
            jax.ShapeDtypeStruct((8, 128), F32),
            jax.ShapeDtypeStruct((rows, width), BF16),
            jax.ShapeDtypeStruct((64, 128), F32),
        ),
        in_specs=[pl.BlockSpec(memory_space=pltpu.SMEM), hbm, hbm, hbm],
        out_specs=(vmem, hbm, vmem),
        scratch_shapes=scratch,
        compiler_params=pltpu.CompilerParams(
            collective_id=0, has_side_effects=True, vmem_limit_bytes=60 * 1024 * 1024
        ),
        name="distill",
    )(draft_list, hidden.reshape(rows, width), teacher_weight, draft_weight)
    loss, grad_hidden, grad_draft = pl.pallas_call(
        functools.partial(deliver, tiles),
        out_shape=(
            jax.ShapeDtypeStruct((tiles, tile_rows), F32),
            jax.ShapeDtypeStruct((rows, width), BF16),
            jax.ShapeDtypeStruct((64, 128), F32),
        ),
        in_specs=[hbm, hbm, hbm],
        out_specs=(hbm, hbm, hbm),
        scratch_shapes=[
            pltpu.VMEM((8, 128), F32), pltpu.VMEM((tiles, tile_rows), F32), pltpu.VMEM((rows, width), BF16),
            pltpu.VMEM((64, 128), F32), dma((CHUNKS + 2,)), dma((CHUNKS + 2,)),
        ],
        compiler_params=pltpu.CompilerParams(vmem_limit_bytes=60 * 1024 * 1024),
        name="deliver",
    )(loss, grad_hidden, grad_draft)
    return loss, grad_hidden.reshape(hidden.shape), grad_draft


def solution(mesh):
    nx, devices = mesh.shape["vocab"], mesh.shape["rows"]
    ring = int(round((devices // 2) ** 0.5))
    in_specs = (P(None, "rows", None), P("rows", "vocab"), P("rows", "vocab"), P())
    out_specs = (P(None, "rows"), P(None, "rows", None), P("rows", "vocab"))
    return jax.shard_map(
        functools.partial(per_device, nx, ring), mesh=mesh, in_specs=in_specs, out_specs=out_specs, check_vma=False
    )
```

```python
import functools
import heapq

import jax
import jax.numpy as jnp
from jax import lax
from jax.experimental import pallas as pl
from jax.experimental.pallas import tpu as pltpu
from jax.sharding import PartitionSpec as P

CHUNKS = 8
F32 = jnp.float32
BF16 = jnp.bfloat16
MESH = pl.DeviceIdType.MESH
NT = (((1,), (1,)), ((), ()))


def offset_of(k):
    return 0 if k == 0 else (-(k + 1) // 2 if k % 2 else k // 2)


def reach(ring, kind, k):
    half = ring // 2
    if kind == "P" or k % 2 == 0:
        return {"R": half, "L": half - 1}
    return {"R": half - 1, "L": half}


def follow(ring, event):
    kind, k, way, dist = event
    sends = []
    if kind == "P":
        if way is None:
            sends += [("P", 0, w, 1) for w in "RL" if reach(ring, "P", 0)[w] >= 1]
            first = 0
        else:
            if dist < reach(ring, "P", 0)[way]:
                sends.append(("P", 0, way, dist + 1))
            first = 2 * dist - 1 if way == "R" else 2 * dist
        sends += [("Q", first, w, 1) for w in "RL" if reach(ring, "Q", first)[w] >= 1]
    elif dist < reach(ring, "Q", k)[way]:
        sends.append(("Q", k, way, dist + 1))
    return sends


def event_order(ring, slab_us=0.7, hop_us=1.7, step_us=0.2):
    free = {"R": 0.0, "L": 0.0}
    arrivals, order, now, count = [], [], 0.0, 0
    pending = [("P", 0, None, 0)]
    while True:
        for event in pending:
            for sent in follow(ring, event):
                way = sent[2]
                free[way] = max(free[way], now) + slab_us
                count += 1
                heapq.heappush(arrivals, (free[way] + hop_us, count, sent))
        if not arrivals:
            return order
        when, _, event = heapq.heappop(arrivals)
        now = max(now + step_us, when)
        order.append(event)
        pending = [event]


def kernel(
    nx, ring, list_ref, hid_ref, tw_ref, dw_ref, loss_ref, gh_ref, gd_ref,
    wbuf, hb, acc, full, dall, dq, msg, msgr, stm, stmr, eown, lgall, crs, crsr, rss, rsr, rso, fsd, fin, ghs,
    init_sem, hid_sem, ag_send, ag_recv, xg_send, xg_recv, xr_send, dq_send, dq_recv, lx_send, lx_recv, sm_send, sm_recv, st_send, st_recv,
    lg_send, lg_recv, cr_send, cr_recv, rs_send, rs_recv, f_send, f_recv, gh_send, gh_recv, gh_loc,
    gx_send, gx_recv, gy_send,
):
    x = lax.axis_index("vocab")
    r = lax.axis_index("rows")
    c = lax.rem(r, 2)
    chip = r // 2
    y, z = chip // ring, lax.rem(chip, ring)
    p = y + c * (z - y)
    q = z + c * (y - z)
    half = ring // 2
    whole = half // 2
    part = ring // nx

    def mod(v):
        return lax.rem(v + 2 * ring, ring)

    def xmod(v):
        return lax.rem(v + nx, nx)

    def chip_of(pp, qq):
        straight, turned = pp * ring + qq, qq * ring + pp
        return straight + c * (turned - straight)

    def at(pp, qq):
        return (x, chip_of(mod(pp), mod(qq)) * 2 + c)

    partner = (x, chip * 2 + 1 - c)

    def rcopy(src, dst, ssem, rsem, dev):
        return pltpu.make_async_remote_copy(
            src_ref=src, dst_ref=dst, send_sem=ssem, recv_sem=rsem, device_id=dev, device_id_type=MESH
        )

    hid_local = pltpu.make_async_copy(hid_ref, hb.at[0:128], hid_sem.at[0])
    own = wbuf.at[y, z]
    loc_a0 = pltpu.make_async_copy(tw_ref.at[:, 0:256], own.at[0:64, :], init_sem.at[0])
    loc_b1 = pltpu.make_async_copy(tw_ref.at[:, 256:384], own.at[64:128, 0:128], init_sem.at[0])
    loc_b2 = pltpu.make_async_copy(dw_ref, own.at[64:128, 128:256], init_sem.at[1])

    @pl.when(c == 0)
    def _():
        loc_a0.start()

    @pl.when(c == 1)
    def _():
        loc_b1.start()
        loc_b2.start()

    hid_local.start()

    barrier = pltpu.get_barrier_semaphore()
    greeted = 0
    for d in range(1, ring):
        for core in (0, 1):
            for dev in ((mod(y + d) * ring + z), (y * ring + mod(z + d))):
                pl.semaphore_signal(barrier, inc=1, device_id=(x, dev * 2 + core), device_id_type=MESH)
                greeted += 1
    for d in range(1, nx):
        for core in (0, 1):
            pl.semaphore_signal(barrier, inc=1, device_id=(xmod(x + d), chip * 2 + core), device_id_type=MESH)
            greeted += 1
    pl.semaphore_signal(barrier, inc=1, device_id=partner, device_id_type=MESH)
    pl.semaphore_wait(barrier, greeted + 1)

    to_b1 = rcopy(tw_ref.at[:, 256:384], own.at[0:64, 0:128], init_sem.at[2], init_sem.at[4], partner)
    to_b2 = rcopy(dw_ref, own.at[0:64, 128:256], init_sem.at[3], init_sem.at[5], partner)
    to_a = rcopy(tw_ref.at[:, 0:256], own.at[64:128, :], init_sem.at[2], init_sem.at[4], partner)
    from_a1 = rcopy(tw_ref.at[:, 256:384], own.at[0:64, 0:128], init_sem.at[2], init_sem.at[4], partner)
    from_a2 = rcopy(dw_ref, own.at[0:64, 128:256], init_sem.at[3], init_sem.at[5], partner)
    from_b = rcopy(tw_ref.at[:, 0:256], own.at[64:128, :], init_sem.at[2], init_sem.at[4], partner)

    @pl.when(c == 0)
    def _():
        to_b1.start()
        to_b2.start()

    @pl.when(c == 1)
    def _():
        to_a.start()

    hid_out = rcopy(hid_ref, hb.at[128:256], hid_sem.at[1], hid_sem.at[2], partner)
    hid_out.start()

    @pl.when(c == 0)
    def _():
        loc_a0.wait()
        from_b.wait_recv()

    @pl.when(c == 1)
    def _():
        loc_b1.wait()
        loc_b2.wait()
        from_a1.wait_recv()
        from_a2.wait_recv()

    events = event_order(ring)
    number = {event: i for i, event in enumerate(events)}

    def slab_pos(net, event):
        kind, k, way, dist = event
        step = -dist if way == "R" else dist
        first, second = (step, 0) if kind == "P" else (offset_of(k), step)
        return (mod(y + first), mod(z + second)) if net == 0 else (mod(y + second), mod(z + first))

    def half_slab(net, pos):
        return wbuf.at[pos[0], pos[1], :, 128 * net:128 * net + 128]

    def send_along(net, sent, pos):
        kind, _, way, _ = sent
        step = 1 if way == "R" else -1
        if (kind == "P") == (net == 0):
            dev = mod(y + step) * ring + z
        else:
            dev = y * ring + mod(z + step)
        i = number[sent]
        slab = half_slab(net, pos)
        rcopy(slab, slab, ag_send.at[net, i], ag_recv.at[net, i], (x, dev * 2 + c)).start()

    def multiply(net, pos):
        yy, zz = pos
        lanes = pl.ds(pl.multiple_of((yy * ring + zz) * 128, 128), 128)
        columns = slice(128 * net, 128 * net + 128)
        acc[:, columns] += jnp.dot(hb[:, lanes], wbuf[yy, zz, :, columns], preferred_element_type=F32)

    def class_of(event):
        kind, k, way, dist = event
        if kind == "P":
            return (0, 0)
        if dist == half:
            return (1, half - 1)
        return (0, dist) if way == "L" else (1, dist - 1)

    left_in_class = {}
    for event in events:
        left_in_class[class_of(event)] = left_in_class.get(class_of(event), 0) + 1

    def class_y(h, i):
        return mod(y + i - h * (1 + 2 * i))

    def x_copies(h, i):
        src = wbuf.at[class_y(h, i), :, :, 128:256]
        dst = dall.at[x, i]
        out = []
        if nx > 1:
            out.append(rcopy(src, dst, xg_send.at[h, i, 0], xg_recv.at[0, i], (xmod(x + 1), chip * 2 + h)))
            out.append(rcopy(src, dst, xg_send.at[h, i, 1], xg_recv.at[1, i], (xmod(x - 1), chip * 2 + h)))
        if h == 0:
            out.append(rcopy(src, dst, xg_send.at[h, i, 2], xg_recv.at[3, i], (x, chip * 2)))
        else:
            out.append(pltpu.make_async_copy(src, dst, xg_recv.at[3, i]))
        return out

    def dq_copies(h, i):
        out = []
        for d in range(nx):
            xx = xmod(x + d)
            src = wbuf.at[class_y(h, i), pl.ds(part * xx, part), :, 128:256]
            dst = dq.at[x, i - whole]
            if d == 0 and h == 1:
                out.append(pltpu.make_async_copy(src, dst, dq_recv.at[0, i - whole]))
            else:
                dev = (xx, chip * 2 + h)
                out.append(rcopy(src, dst, dq_send.at[h, i - whole, d], dq_recv.at[d, i - whole], dev))
        return out

    def x_start(h, i):
        @pl.when(c == 1)
        def _():
            for copy in x_copies(h, i) if i < whole else dq_copies(h, i):
                copy.start()

    def x_arrived(kind, i):
        group = {0: xmod(x - 1), 1: xmod(x + 1), 2: xmod(x + 2), 3: x}[kind]
        slot = dall.at[group, i]
        return rcopy(slot, slot, xr_send.at[i], xg_recv.at[kind, i], (xmod(x + 1), r))

    def x_relay(i):
        if nx == 4:
            kind = i % 2
            x_arrived(kind, i).wait_recv()
            group = xmod(x - 1) if kind == 0 else xmod(x + 1)
            dev = (xmod(x + 1), r) if kind == 0 else (xmod(x - 1), r)
            slot = dall.at[group, i]
            rcopy(slot, slot, xr_send.at[i], xg_recv.at[2, i], dev).start()

    for sent in follow(ring, ("P", 0, None, 0)):
        for net in (0, 1):
            send_along(net, sent, (y, z))
    acc[...] = jnp.zeros_like(acc)

    todo = [(0, (y, z)), (1, (y, z))]
    have_hidden = False
    held = []
    relay_at = {}
    for n, event in enumerate(events):
        for net in (0, 1):
            pos = slab_pos(net, event)
            slab = half_slab(net, pos)
            rcopy(slab, slab, ag_send.at[net, n], ag_recv.at[net, n], partner).wait_recv()
            for sent in follow(ring, event):
                send_along(net, sent, pos)
            todo.append((net, pos))
        cls = class_of(event)
        left_in_class[cls] -= 1
        if left_in_class[cls] == 0:
            if cls[1] < whole:
                x_start(*cls)
                relay_at.setdefault(n + 16, []).append(cls)
            else:
                held.append(cls)
        for h, i in relay_at.pop(n, ()):
            pl.when(c == h)(functools.partial(x_relay, i))
        if n >= min(10, len(events) - 1):
            if not have_hidden:
                hid_local.wait()
                hid_out.wait_recv()
                have_hidden = True
            for _ in range(min(4, len(todo))):
                multiply(*todo.pop(0))
    for job in todo:
        multiply(*job)

    cols = pl.ds(pl.multiple_of(c * 256, 256), 256)
    lx = rcopy(acc.at[128:256], full.at[:, cols], lx_send, lx_recv, partner)
    lx.start()
    full[:, cols] = acc[0:128, :]
    other = full.at[:, pl.ds(pl.multiple_of((1 - c) * 256, 256), 256)]
    rcopy(other, other, lx_send, lx_recv, partner).wait_recv()

    t_logits = full[:, 0:384]
    d_logits = full[:, 384:512]
    t_max = jnp.max(t_logits, axis=1, keepdims=True)
    t_exp = jnp.exp(t_logits - t_max)
    t_sum = jnp.sum(t_exp, axis=1, keepdims=True)

    def sm_copy(d):
        return rcopy(msg.at[d - 1], msgr.at[d - 1], sm_send.at[d - 1], sm_recv.at[d - 1], (xmod(x + d), r))

    def st_copy(d):
        return rcopy(stm, stmr.at[d - 1], st_send.at[d - 1], st_recv.at[d - 1], (xmod(x + d), r))

    totals = [jnp.zeros((32, 128), F32) for _ in range(4)]
    for d in sorted(range(nx), key=lambda d: -min(d, nx - d)):
        for t in range(4):
            rows = slice(32 * t, 32 * t + 32)
            wanted = list_ref[t, xmod(x + d)]
            piece = jnp.zeros((32, 128), F32)
            for b in range(3):
                keep = jnp.where(wanted == 3 * x + b, 1.0, 0.0).astype(F32)
                piece += keep * t_exp[rows, 128 * b:128 * b + 128]
            if d == 0:
                eown[rows, :] = piece
            else:
                msg[d - 1, rows, :] = piece.astype(BF16)
            totals[t] += piece
        if d > 0:
            sm_copy(d).start()
    cover = jnp.concatenate([jnp.sum(total, axis=1, keepdims=True) for total in totals], axis=0)
    d_max = jnp.max(d_logits, axis=1, keepdims=True)
    d_sum = jnp.sum(jnp.exp(d_logits - d_max), axis=1, keepdims=True)
    lane = lax.broadcasted_iota(jnp.int32, (128, 128), 1)
    stats = jnp.zeros((128, 128), F32)
    for i, value in enumerate((t_max, t_sum, cover, d_max, d_sum)):
        stats = jnp.where(lane == i, value, stats)
    stm[...] = stats.T[0:8, :]
    for d in range(1, nx):
        st_copy(d).start()
    for cls in held:
        x_start(*cls)
    for n in sorted(relay_at):
        for h, i in relay_at[n]:
            pl.when(c == h)(functools.partial(x_relay, i))
    for d in range(1, nx):
        st_copy(d).wait_recv()
    stat = [(t_max, t_sum, cover, d_max, d_sum)]
    for d in range(1, nx):
        got = jnp.concatenate([stmr[d - 1]] * 16, axis=0).T
        stat.append(tuple(got[:, i:i + 1] for i in range(5)))
    all_tmax = functools.reduce(jnp.maximum, [s[0] for s in stat])
    all_dmax = functools.reduce(jnp.maximum, [s[3] for s in stat])
    t_scale = [jnp.exp(s[0] - all_tmax) for s in stat]
    all_tsum = sum(s[1] * a for s, a in zip(stat, t_scale))
    all_dsum = sum(s[4] * jnp.exp(s[3] - all_dmax) for s in stat)
    covered = sum(s[2] * a for s, a in zip(stat, t_scale)) / all_tsum
    target = eown[...] * (t_scale[0] / all_tsum)
    prob = jnp.exp(d_logits - all_dmax) / all_dsum
    for d in range(1, nx):
        sm_copy(d).wait_recv()
        target += msgr[d - 1].astype(F32) * (t_scale[d] / all_tsum)
    lgall[x, 0:128, :] = (covered * prob - target).astype(BF16)

    def lg_copies():
        src = lgall.at[x, 0:128]
        out = [rcopy(src, lgall.at[x, 128:256], lg_send.at[0, 1], lg_recv.at[0, 1], partner)]
        for d in range(1, nx):
            xx = xmod(x + d)
            out.append(rcopy(src, lgall.at[x, 0:128], lg_send.at[d, 0], lg_recv.at[d, 0], (xx, r)))
            out.append(
                rcopy(src, lgall.at[x, 128:256], lg_send.at[d, 1], lg_recv.at[d, 1], (xx, chip * 2 + 1 - c))
            )
        return out

    def lg_wait(d, side):
        group = xmod(x - d)
        slot = lgall.at[group, 128 * side:128 * side + 128]
        rcopy(slot, slot, lg_send.at[d, side], lg_recv.at[d, side], partner).wait_recv()

    for copy in lg_copies():
        copy.start()
    crossed = jnp.sum(target * d_logits, axis=1, keepdims=True)
    crs[...] = jnp.broadcast_to(crossed, (128, 128)).T[0:8, :]

    def cr_copy(d):
        return rcopy(crs, crsr.at[d - 1], cr_send.at[d - 1], cr_recv.at[d - 1], (xmod(x + d), r))

    for d in range(1, nx):
        cr_copy(d).start()

    lg_wait(0, 1)
    lg_t = lgall[x].astype(F32).T.astype(BF16)
    odd = lax.rem(p + q + c, 2)

    def partial(pp, i):
        qq = 2 * i + lax.rem(pp + c, 2)
        lanes = pl.ds(pl.multiple_of(chip_of(pp, qq) * 128, 128), 128)
        return jnp.dot(lg_t, hb[:, lanes], preferred_element_type=F32)

    def rs_copy(d):
        return rcopy(rss.at[d - 1], rsr.at[d - 1], rs_send.at[d - 1], rs_recv.at[d - 1], at(p + d, q))

    for d in sorted(range(1, ring), key=lambda d: -min(d, ring - d)):
        for i in range(half):
            rss[d - 1, i] = partial(mod(p + d), i).astype(BF16)
        rs_copy(d).start()
    for i in range(half):
        rso[i] = partial(p, i)

    loss = covered * (all_dmax + jnp.log(all_dsum))
    loss_row = jnp.broadcast_to(loss, (128, 128)).T[0:8, :] - crs[...]
    for d in range(1, nx):
        cr_copy(d).wait_recv()
        loss_row -= crsr[d - 1]
    loss_ref[...] = loss_row

    for d in range(1, nx):
        for side in (0, 1):
            lg_wait(d, side)

    wide = ring * 128
    piece_wide = part * 128

    def gh_lanes(h, i, xx):
        if i < whole:
            return pl.ds(pl.multiple_of(class_y(h, i) * wide, wide), wide)
        return pl.ds(pl.multiple_of(class_y(h, i) * wide + xx * piece_wide, piece_wide), piece_wide)

    def gh_src(i, side):
        return ghs.at[i, 128 * side:128 * side + 128, 0:wide if i < whole else piece_wide]

    def gh_copies(i):
        lanes = gh_lanes(c, i, x)
        mine = pltpu.make_async_copy(gh_src(i, 0), gh_ref.at[:, lanes], gh_loc.at[i])
        theirs = rcopy(gh_src(i, 1), gh_ref.at[:, lanes], gh_send.at[i], gh_recv.at[i], partner)
        return mine, theirs

    def gx_copies(i):
        out = []
        if nx > 1:
            lanes = gh_lanes(c, i, x)
            for side in (0, 1):
                core = chip * 2 + (c if side == 0 else 1 - c)
                for kind, xx in ((0, xmod(x + 1)), (1, xmod(x - 1))):
                    out.append(
                        rcopy(
                            gh_src(i, side), gh_ref.at[:, lanes], gx_send.at[side, i - whole, kind],
                            gx_recv.at[side, i - whole, kind], (xx, core),
                        )
                    )
        return out

    def gx_arrived(side, i, kind):
        h = c if side == 0 else 1 - c
        xx = {0: xmod(x - 1), 1: xmod(x + 1), 2: xmod(x + 2)}[kind]
        slot = gh_ref.at[:, gh_lanes(h, i, xx)]
        return rcopy(slot, slot, gy_send.at[side, i - whole], gx_recv.at[side, i - whole, kind], (xmod(x + 1), r))

    def gx_relay(side, i):
        kind = (i - whole) % 2
        gx_arrived(side, i, kind).wait_recv()
        h = c if side == 0 else 1 - c
        slot = gh_ref.at[:, gh_lanes(h, i, xmod(x - 1) if kind == 0 else xmod(x + 1))]
        dev = (xmod(x + 1) if kind == 0 else xmod(x - 1), r)
        rcopy(slot, slot, gy_send.at[side, i - whole], gx_recv.at[side, i - whole, 2], dev).start()

    for i in range(whole, half):
        for d in range(nx):
            slot = dq.at[xmod(x - d), i - whole]
            if d == 0:
                @pl.when(c == 1)
                def _():
                    dq_copies(1, i)[0].wait()

                @pl.when(c == 0)
                def _():
                    rcopy(slot, slot, dq_send.at[0, 0, 0], dq_recv.at[0, i - whole], partner).wait_recv()
            else:
                rcopy(slot, slot, dq_send.at[0, 0, 0], dq_recv.at[d, i - whole], partner).wait_recv()

        for s in range(part):
            summed = jnp.zeros((256, 128), F32)
            for g in range(nx):
                piece = lax.dot_general(lgall[g], dq[g, i - whole, s], NT, preferred_element_type=F32)
                summed += piece.astype(BF16).astype(F32)
            ghs[i, :, 128 * s:128 * s + 128] = summed.astype(BF16)
        for copy in (*gx_copies(i), *gh_copies(i)):
            copy.start()

    for i in range(whole):
        if nx > 1:
            for kind in (0, 1, 2):
                if kind == i % 2:
                    continue
                x_arrived(kind, i).wait_recv()

        @pl.when(c == 0)
        def _():
            x_arrived(3, i).wait_recv()

        @pl.when(c == 1)
        def _():
            pltpu.make_async_copy(wbuf.at[class_y(1, i), :, :, 128:256], dall.at[x, i], xg_recv.at[3, i]).wait()

        def width(s, carry):
            summed = jnp.zeros((256, 128), F32)
            for g in range(nx):
                piece = lax.dot_general(lgall[g], dall[g, i, s], NT, preferred_element_type=F32)
                summed += piece.astype(BF16).astype(F32)
            ghs[i, :, pl.ds(pl.multiple_of(s * 128, 128), 128)] = summed.astype(BF16)
            return carry

        lax.fori_loop(0, ring, width, 0)
        for copy in gh_copies(i):
            copy.start()

    for d in range(1, ring):
        rs_copy(d).wait_recv()

    def add_up(i, carry):
        total = rso[i]
        for d in range(1, ring):
            total += rsr[d - 1, i].astype(F32)
        fsd[i] = total.T.astype(BF16)
        return carry

    lax.fori_loop(0, half, add_up, 0)

    def f_copy(i, core):
        d = odd + 2 * i
        qq = mod(q + d)
        j = (qq - lax.rem(p + c, 2)) // 2
        dev = (x, chip_of(p, qq) * 2 + core)
        return rcopy(
            fsd.at[j, 64 * core:64 * core + 64], fin.at[d], f_send.at[i, core], f_recv.at[d], dev
        )

    def f_stays(i, core):
        return jnp.logical_and(odd + 2 * i == 0, core == c)

    for i in range(half):
        for core in (0, 1):
            stays = f_stays(i, core)

            @pl.when(jnp.logical_not(stays))
            def _():
                f_copy(i, core).start()

            @pl.when(stays)
            def _():
                j = (q - lax.rem(p + c, 2)) // 2
                fin[0] = fsd[j, 64 * core:64 * core + 64, :]

    if nx == 4:
        for i in range(whole, half):
            for side in (0, 1):
                gx_relay(side, i)

    home = lax.rem(y + z + c, 2) == 0
    grad = jnp.zeros((64, 128), F32)
    for d in range(ring):
        slot = fin.at[d]
        arrival = rcopy(slot, slot, f_send.at[0, 0], f_recv.at[d], partner)
        if d == 0:
            pl.when(jnp.logical_not(home))(arrival.wait_recv)
        else:
            arrival.wait_recv()
        grad += fin[d].astype(F32)
    gd_ref[...] = grad

    for i in range(half):
        mine, theirs = gh_copies(i)
        mine.wait()
        theirs.wait_send()
    for i in range(half):
        slot = gh_ref.at[:, gh_lanes(1 - c, i, x)]
        rcopy(slot, slot, gh_send.at[i], gh_recv.at[i], partner).wait_recv()
    if nx == 4:
        for i in range(whole, half):
            for side in (0, 1):
                for kind in (0, 1, 2):
                    if kind != (i - whole) % 2:
                        gx_arrived(side, i, kind).wait_recv()
                gx_arrived(side, i, 0).wait_send()
            for copy in gx_copies(i):
                copy.wait_send()
    for i in range(half):
        for core in (0, 1):
            @pl.when(jnp.logical_not(f_stays(i, core)))
            def _():
                f_copy(i, core).wait_send()
    for d in range(1, ring):
        rs_copy(d).wait_send()
    for d in range(1, nx):
        cr_copy(d).wait_send()
        sm_copy(d).wait_send()
        st_copy(d).wait_send()
    for copy in lg_copies():
        copy.wait_send()
    lx.wait_send()
    hid_out.wait_send()

    @pl.when(c == 0)
    def _():
        to_b1.wait_send()
        to_b2.wait_send()

    @pl.when(c == 1)
    def _():
        to_a.wait_send()
        for h in (0, 1):
            for i in range(whole):
                for n, copy in enumerate(x_copies(h, i)):
                    if nx > 1 and n < 2 or h == 0:
                        copy.wait_send()
            for i in range(whole, half):
                for d, copy in enumerate(dq_copies(h, i)):
                    if d > 0 or h == 0:
                        copy.wait_send()

    if nx == 4:
        for i in range(whole):
            x_arrived(0, i).wait_send()
    for n, event in enumerate(events):
        for net in (0, 1):
            slab = half_slab(net, (0, 0))
            rcopy(slab, slab, ag_send.at[net, n], ag_recv.at[net, n], partner).wait_send()


def deliver(tiles, loss_in, gh_in, gd_in, loss_out, gh_out, gd_out, wide_loss, loss_buf, gh_buf, gd_buf, come, go):
    rows = gh_in.shape[0] // CHUNKS
    chunks = [slice(rows * n, rows * n + rows) for n in range(CHUNKS)]
    take_loss = pltpu.make_async_copy(loss_in, wide_loss, come.at[CHUNKS])
    take_gd = pltpu.make_async_copy(gd_in, gd_buf, come.at[CHUNKS + 1])
    put_loss = pltpu.make_async_copy(loss_buf, loss_out, go.at[CHUNKS])
    put_gd = pltpu.make_async_copy(gd_buf, gd_out, go.at[CHUNKS + 1])
    take = [pltpu.make_async_copy(gh_in.at[k], gh_buf.at[k], come.at[n]) for n, k in enumerate(chunks)]
    put = [pltpu.make_async_copy(gh_buf.at[k], gh_out.at[k], go.at[n]) for n, k in enumerate(chunks)]
    for copy in (take_loss, take_gd, *take):
        copy.start()
    take_loss.wait()
    lanes = loss_buf.shape[1]
    for t in range(tiles):
        loss_buf[t:t + 1, :] = wide_loss[0:1, lanes * t:lanes * t + lanes]
    put_loss.start()
    take_gd.wait()
    put_gd.start()
    for taken, given in zip(take, put):
        taken.wait()
        given.start()
    for copy in (put_loss, put_gd, *put):
        copy.wait()


def per_device(nx, ring, hidden, teacher_weight, draft_weight, draft_list):
    tiles, tile_rows, width = hidden.shape
    rows = tiles * tile_rows
    half = ring // 2
    whole = half // 2
    parts = half - whole
    dma = pltpu.SemaphoreType.DMA
    more = max(nx - 1, 1)
    scratch = [
        pltpu.VMEM((ring, ring, 128, 256), BF16),
        pltpu.VMEM((2 * rows, width), BF16),
        pltpu.VMEM((2 * rows, 256), F32),
        pltpu.VMEM((rows, 512), F32),
        pltpu.VMEM((nx, max(whole, 1), ring, 128, 128), BF16),
        pltpu.VMEM((nx, half - whole, ring // nx, 128, 128), BF16),
        pltpu.VMEM((more, rows, 128), BF16),
        pltpu.VMEM((more, rows, 128), BF16),
        pltpu.VMEM((8, 128), F32),
        pltpu.VMEM((more, 8, 128), F32),
        pltpu.VMEM((rows, 128), F32),
        pltpu.VMEM((nx, 2 * rows, 128), BF16),
        pltpu.VMEM((8, 128), F32),
        pltpu.VMEM((more, 8, 128), F32),
        pltpu.VMEM((ring - 1, half, 128, 128), BF16),
        pltpu.VMEM((ring - 1, half, 128, 128), BF16),
        pltpu.VMEM((half, 128, 128), F32),
        pltpu.VMEM((half, 128, 128), BF16),
        pltpu.VMEM((ring, 64, 128), BF16),
        pltpu.VMEM((half, 2 * rows, ring * 128), BF16),
        dma((6,)), dma((3,)), dma((2, ring * ring)), dma((2, ring * ring)),
        dma((2, half, 3)), dma((4, half)), dma((half,)), dma((2, parts, nx)), dma((nx, parts)),
        dma(()), dma(()), dma((more,)), dma((more,)), dma((more,)), dma((more,)),
        dma((nx, 2)), dma((nx, 2)), dma((more,)), dma((more,)),
        dma((ring - 1,)), dma((ring - 1,)), dma((half, 2)), dma((ring,)),
        dma((half,)), dma((half,)), dma((half,)),
        dma((2, parts, 2)), dma((2, parts, 3)), dma((2, parts)),
    ]
    hbm = pl.BlockSpec(memory_space=pl.ANY)
    vmem = pl.BlockSpec(memory_space=pltpu.VMEM)
    loss, grad_hidden, grad_draft = pl.pallas_call(
        functools.partial(kernel, nx, ring),
        out_shape=(
            jax.ShapeDtypeStruct((8, 128), F32),
            jax.ShapeDtypeStruct((rows, width), BF16),
            jax.ShapeDtypeStruct((64, 128), F32),
        ),
        in_specs=[pl.BlockSpec(memory_space=pltpu.SMEM), hbm, hbm, hbm],
        out_specs=(vmem, hbm, vmem),
        scratch_shapes=scratch,
        compiler_params=pltpu.CompilerParams(
            collective_id=0, has_side_effects=True, vmem_limit_bytes=60 * 1024 * 1024
        ),
        name="distill",
    )(draft_list, hidden.reshape(rows, width), teacher_weight, draft_weight)
    loss, grad_hidden, grad_draft = pl.pallas_call(
        functools.partial(deliver, tiles),
        out_shape=(
            jax.ShapeDtypeStruct((tiles, tile_rows), F32),
            jax.ShapeDtypeStruct((rows, width), BF16),
            jax.ShapeDtypeStruct((64, 128), F32),
        ),
        in_specs=[hbm, hbm, hbm],
        out_specs=(hbm, hbm, hbm),
        scratch_shapes=[
            pltpu.VMEM((8, 128), F32), pltpu.VMEM((tiles, tile_rows), F32), pltpu.VMEM((rows, width), BF16),
            pltpu.VMEM((64, 128), F32), dma((CHUNKS + 2,)), dma((CHUNKS + 2,)),
        ],
        compiler_params=pltpu.CompilerParams(vmem_limit_bytes=60 * 1024 * 1024),
        name="deliver",
    )(loss, grad_hidden, grad_draft)
    return loss, grad_hidden.reshape(hidden.shape), grad_draft


def solution(mesh):
    nx, devices = mesh.shape["vocab"], mesh.shape["rows"]
    ring = int(round((devices // 2) ** 0.5))
    in_specs = (P(None, "rows", None), P("rows", "vocab"), P("rows", "vocab"), P())
    out_specs = (P(None, "rows"), P(None, "rows", None), P("rows", "vocab"))
    return jax.shard_map(
        functools.partial(per_device, nx, ring), mesh=mesh, in_specs=in_specs, out_specs=out_specs, check_vma=False
    )
```

```python
import functools
import heapq

import jax
import jax.numpy as jnp
from jax import lax
from jax.experimental import pallas as pl
from jax.experimental.pallas import tpu as pltpu
from jax.sharding import PartitionSpec as P

CHUNKS = 8
F32 = jnp.float32
BF16 = jnp.bfloat16
MESH = pl.DeviceIdType.MESH
NT = (((1,), (1,)), ((), ()))


def offset_of(k):
    return 0 if k == 0 else (-(k + 1) // 2 if k % 2 else k // 2)


def reach(ring, kind, k):
    half = ring // 2
    if kind == "P" or k % 2 == 0:
        return {"R": half, "L": half - 1}
    return {"R": half - 1, "L": half}


def follow(ring, event):
    kind, k, way, dist = event
    sends = []
    if kind == "P":
        if way is None:
            sends += [("P", 0, w, 1) for w in "RL" if reach(ring, "P", 0)[w] >= 1]
            first = 0
        else:
            if dist < reach(ring, "P", 0)[way]:
                sends.append(("P", 0, way, dist + 1))
            first = 2 * dist - 1 if way == "R" else 2 * dist
        sends += [("Q", first, w, 1) for w in "RL" if reach(ring, "Q", first)[w] >= 1]
    elif dist < reach(ring, "Q", k)[way]:
        sends.append(("Q", k, way, dist + 1))
    return sends


def event_order(ring, slab_us=0.7, hop_us=1.7, step_us=0.2):
    free = {"R": 0.0, "L": 0.0}
    arrivals, order, now, count = [], [], 0.0, 0
    pending = [("P", 0, None, 0)]
    while True:
        for event in pending:
            for sent in follow(ring, event):
                way = sent[2]
                free[way] = max(free[way], now) + slab_us
                count += 1
                heapq.heappush(arrivals, (free[way] + hop_us, count, sent))
        if not arrivals:
            return order
        when, _, event = heapq.heappop(arrivals)
        now = max(now + step_us, when)
        order.append(event)
        pending = [event]


def kernel(
    nx, ring, list_ref, hid_ref, tw_ref, dw_ref, loss_ref, gh_ref, gd_ref,
    wbuf, hb, acc, full, dall, dq, msg, msgr, stm, stmr, eown, lgall, crs, crsr, rss, rsr, rso, fsd, fin, ghs,
    init_sem, hid_sem, ag_send, ag_recv, xg_send, xg_recv, xr_send, dq_send, dq_recv, lx_send, lx_recv, sm_send, sm_recv, st_send, st_recv,
    lg_send, lg_recv, cr_send, cr_recv, rs_send, rs_recv, f_send, f_recv, gh_send, gh_recv, gh_loc,
    gx_send, gx_recv, gy_send,
):
    x = lax.axis_index("vocab")
    r = lax.axis_index("rows")
    c = lax.rem(r, 2)
    chip = r // 2
    y, z = chip // ring, lax.rem(chip, ring)
    p = y + c * (z - y)
    q = z + c * (y - z)
    half = ring // 2
    whole = half // 2
    part = ring // nx

    def mod(v):
        return lax.rem(v + 2 * ring, ring)

    def xmod(v):
        return lax.rem(v + nx, nx)

    def chip_of(pp, qq):
        straight, turned = pp * ring + qq, qq * ring + pp
        return straight + c * (turned - straight)

    def at(pp, qq):
        return (x, chip_of(mod(pp), mod(qq)) * 2 + c)

    partner = (x, chip * 2 + 1 - c)

    def rcopy(src, dst, ssem, rsem, dev):
        return pltpu.make_async_remote_copy(
            src_ref=src, dst_ref=dst, send_sem=ssem, recv_sem=rsem, device_id=dev, device_id_type=MESH
        )

    hid_local = pltpu.make_async_copy(hid_ref, hb.at[0:128], hid_sem.at[0])
    own = wbuf.at[y, z]
    loc_a0 = pltpu.make_async_copy(tw_ref.at[:, 0:256], own.at[0:64, :], init_sem.at[0])
    loc_b1 = pltpu.make_async_copy(tw_ref.at[:, 256:384], own.at[64:128, 0:128], init_sem.at[0])
    loc_b2 = pltpu.make_async_copy(dw_ref, own.at[64:128, 128:256], init_sem.at[1])

    @pl.when(c == 0)
    def _():
        loc_a0.start()

    @pl.when(c == 1)
    def _():
        loc_b1.start()
        loc_b2.start()

    hid_local.start()

    barrier = pltpu.get_barrier_semaphore()
    greeted = 0
    for d in range(1, ring):
        for core in (0, 1):
            for dev in ((mod(y + d) * ring + z), (y * ring + mod(z + d))):
                pl.semaphore_signal(barrier, inc=1, device_id=(x, dev * 2 + core), device_id_type=MESH)
                greeted += 1
    for d in range(1, nx):
        for core in (0, 1):
            pl.semaphore_signal(barrier, inc=1, device_id=(xmod(x + d), chip * 2 + core), device_id_type=MESH)
            greeted += 1
    pl.semaphore_signal(barrier, inc=1, device_id=partner, device_id_type=MESH)
    pl.semaphore_wait(barrier, greeted + 1)

    to_b1 = rcopy(tw_ref.at[:, 256:384], own.at[0:64, 0:128], init_sem.at[2], init_sem.at[4], partner)
    to_b2 = rcopy(dw_ref, own.at[0:64, 128:256], init_sem.at[3], init_sem.at[5], partner)
    to_a = rcopy(tw_ref.at[:, 0:256], own.at[64:128, :], init_sem.at[2], init_sem.at[4], partner)
    from_a1 = rcopy(tw_ref.at[:, 256:384], own.at[0:64, 0:128], init_sem.at[2], init_sem.at[4], partner)
    from_a2 = rcopy(dw_ref, own.at[0:64, 128:256], init_sem.at[3], init_sem.at[5], partner)
    from_b = rcopy(tw_ref.at[:, 0:256], own.at[64:128, :], init_sem.at[2], init_sem.at[4], partner)

    @pl.when(c == 0)
    def _():
        to_b1.start()
        to_b2.start()

    @pl.when(c == 1)
    def _():
        to_a.start()

    hid_out = rcopy(hid_ref, hb.at[128:256], hid_sem.at[1], hid_sem.at[2], partner)
    hid_out.start()

    @pl.when(c == 0)
    def _():
        loc_a0.wait()
        from_b.wait_recv()

    @pl.when(c == 1)
    def _():
        loc_b1.wait()
        loc_b2.wait()
        from_a1.wait_recv()
        from_a2.wait_recv()

    events = event_order(ring)
    number = {event: i for i, event in enumerate(events)}

    def slab_pos(net, event):
        kind, k, way, dist = event
        step = -dist if way == "R" else dist
        first, second = (step, 0) if kind == "P" else (offset_of(k), step)
        return (mod(y + first), mod(z + second)) if net == 0 else (mod(y + second), mod(z + first))

    def half_slab(net, pos):
        return wbuf.at[pos[0], pos[1], :, 128 * net:128 * net + 128]

    def send_along(net, sent, pos):
        kind, _, way, _ = sent
        step = 1 if way == "R" else -1
        if (kind == "P") == (net == 0):
            dev = mod(y + step) * ring + z
        else:
            dev = y * ring + mod(z + step)
        i = number[sent]
        slab = half_slab(net, pos)
        rcopy(slab, slab, ag_send.at[net, i], ag_recv.at[net, i], (x, dev * 2 + c)).start()

    def multiply(net, jobs):
        columns = slice(128 * net, 128 * net + 128)
        total = acc[:, columns]
        for yy, zz in jobs:
            lanes = pl.ds(pl.multiple_of((yy * ring + zz) * 128, 128), 128)
            total += jnp.dot(hb[:, lanes], wbuf[yy, zz, :, columns], preferred_element_type=F32)
        acc[:, columns] = total

    def class_of(event):
        kind, k, way, dist = event
        if kind == "P":
            return (0, 0)
        if dist == half:
            return (1, half - 1)
        return (0, dist) if way == "L" else (1, dist - 1)

    left_in_class = {}
    for event in events:
        left_in_class[class_of(event)] = left_in_class.get(class_of(event), 0) + 1

    def class_y(h, i):
        return mod(y + i - h * (1 + 2 * i))

    def x_copies(h, i):
        src = wbuf.at[class_y(h, i), :, :, 128:256]
        dst = dall.at[x, i]
        out = []
        if nx > 1:
            out.append(rcopy(src, dst, xg_send.at[h, i, 0], xg_recv.at[0, i], (xmod(x + 1), chip * 2 + h)))
            out.append(rcopy(src, dst, xg_send.at[h, i, 1], xg_recv.at[1, i], (xmod(x - 1), chip * 2 + h)))
        if h == 0:
            out.append(rcopy(src, dst, xg_send.at[h, i, 2], xg_recv.at[3, i], (x, chip * 2)))
        else:
            out.append(pltpu.make_async_copy(src, dst, xg_recv.at[3, i]))
        return out

    def dq_copies(h, i):
        out = []
        for d in range(nx):
            xx = xmod(x + d)
            src = wbuf.at[class_y(h, i), pl.ds(part * xx, part), :, 128:256]
            dst = dq.at[x, i - whole]
            if d == 0 and h == 1:
                out.append(pltpu.make_async_copy(src, dst, dq_recv.at[0, i - whole]))
            else:
                dev = (xx, chip * 2 + h)
                out.append(rcopy(src, dst, dq_send.at[h, i - whole, d], dq_recv.at[d, i - whole], dev))
        return out

    def x_start(h, i):
        @pl.when(c == 1)
        def _():
            for copy in x_copies(h, i) if i < whole else dq_copies(h, i):
                copy.start()

    def x_arrived(kind, i):
        group = {0: xmod(x - 1), 1: xmod(x + 1), 2: xmod(x + 2), 3: x}[kind]
        slot = dall.at[group, i]
        return rcopy(slot, slot, xr_send.at[i], xg_recv.at[kind, i], (xmod(x + 1), r))

    def x_relay(i):
        if nx == 4:
            kind = i % 2
            x_arrived(kind, i).wait_recv()
            group = xmod(x - 1) if kind == 0 else xmod(x + 1)
            dev = (xmod(x + 1), r) if kind == 0 else (xmod(x - 1), r)
            slot = dall.at[group, i]
            rcopy(slot, slot, xr_send.at[i], xg_recv.at[2, i], dev).start()

    for sent in follow(ring, ("P", 0, None, 0)):
        for net in (0, 1):
            send_along(net, sent, (y, z))
    acc[...] = jnp.zeros_like(acc)

    todo = [[(y, z)], [(y, z)]]
    have_hidden = False
    held = []
    relay_at = {}
    for n, event in enumerate(events):
        for net in (0, 1):
            pos = slab_pos(net, event)
            slab = half_slab(net, pos)
            rcopy(slab, slab, ag_send.at[net, n], ag_recv.at[net, n], partner).wait_recv()
            for sent in follow(ring, event):
                send_along(net, sent, pos)
            todo[net].append(pos)
        cls = class_of(event)
        left_in_class[cls] -= 1
        if left_in_class[cls] == 0:
            if cls[1] < whole:
                x_start(*cls)
                relay_at.setdefault(n + 16, []).append(cls)
            else:
                held.append(cls)
        for h, i in relay_at.pop(n, ()):
            pl.when(c == h)(functools.partial(x_relay, i))
        if n >= min(10, len(events) - 1):
            if not have_hidden:
                hid_local.wait()
                hid_out.wait_recv()
                have_hidden = True
            jobs = todo[n % 2][:4]
            del todo[n % 2][:4]
            if jobs:
                multiply(n % 2, jobs)
    for net in (0, 1):
        if todo[net]:
            multiply(net, todo[net])

    cols = pl.ds(pl.multiple_of(c * 256, 256), 256)
    lx = rcopy(acc.at[128:256], full.at[:, cols], lx_send, lx_recv, partner)
    lx.start()
    full[:, cols] = acc[0:128, :]
    other = full.at[:, pl.ds(pl.multiple_of((1 - c) * 256, 256), 256)]
    rcopy(other, other, lx_send, lx_recv, partner).wait_recv()

    t_logits = full[:, 0:384]
    d_logits = full[:, 384:512]
    t_max = jnp.max(t_logits, axis=1, keepdims=True)
    t_exp = jnp.exp(t_logits - t_max)
    t_sum = jnp.sum(t_exp, axis=1, keepdims=True)

    def sm_copy(d):
        return rcopy(msg.at[d - 1], msgr.at[d - 1], sm_send.at[d - 1], sm_recv.at[d - 1], (xmod(x + d), r))

    def st_copy(d):
        return rcopy(stm, stmr.at[d - 1], st_send.at[d - 1], st_recv.at[d - 1], (xmod(x + d), r))

    totals = [jnp.zeros((32, 128), F32) for _ in range(4)]
    for d in sorted(range(nx), key=lambda d: -min(d, nx - d)):
        for t in range(4):
            rows = slice(32 * t, 32 * t + 32)
            wanted = list_ref[t, xmod(x + d)]
            piece = jnp.zeros((32, 128), F32)
            for b in range(3):
                keep = jnp.where(wanted == 3 * x + b, 1.0, 0.0).astype(F32)
                piece += keep * t_exp[rows, 128 * b:128 * b + 128]
            if d == 0:
                eown[rows, :] = piece
            else:
                msg[d - 1, rows, :] = piece.astype(BF16)
            totals[t] += piece
        if d > 0:
            sm_copy(d).start()
    cover = jnp.concatenate([jnp.sum(total, axis=1, keepdims=True) for total in totals], axis=0)
    d_max = jnp.max(d_logits, axis=1, keepdims=True)
    d_sum = jnp.sum(jnp.exp(d_logits - d_max), axis=1, keepdims=True)
    lane = lax.broadcasted_iota(jnp.int32, (128, 128), 1)
    stats = jnp.zeros((128, 128), F32)
    for i, value in enumerate((t_max, t_sum, cover, d_max, d_sum)):
        stats = jnp.where(lane == i, value, stats)
    stm[...] = stats.T[0:8, :]
    for d in range(1, nx):
        st_copy(d).start()
    for cls in held:
        x_start(*cls)
    for n in sorted(relay_at):
        for h, i in relay_at[n]:
            pl.when(c == h)(functools.partial(x_relay, i))
    for d in range(1, nx):
        st_copy(d).wait_recv()
    stat = [(t_max, t_sum, cover, d_max, d_sum)]
    for d in range(1, nx):
        got = jnp.concatenate([stmr[d - 1]] * 16, axis=0).T
        stat.append(tuple(got[:, i:i + 1] for i in range(5)))
    all_tmax = functools.reduce(jnp.maximum, [s[0] for s in stat])
    all_dmax = functools.reduce(jnp.maximum, [s[3] for s in stat])
    t_scale = [jnp.exp(s[0] - all_tmax) for s in stat]
    all_tsum = sum(s[1] * a for s, a in zip(stat, t_scale))
    all_dsum = sum(s[4] * jnp.exp(s[3] - all_dmax) for s in stat)
    covered = sum(s[2] * a for s, a in zip(stat, t_scale)) / all_tsum
    target = eown[...] * (t_scale[0] / all_tsum)
    prob = jnp.exp(d_logits - all_dmax) / all_dsum
    for d in range(1, nx):
        sm_copy(d).wait_recv()
        target += msgr[d - 1].astype(F32) * (t_scale[d] / all_tsum)
    lgall[x, 0:128, :] = (covered * prob - target).astype(BF16)

    def lg_copies():
        src = lgall.at[x, 0:128]
        out = [rcopy(src, lgall.at[x, 128:256], lg_send.at[0, 1], lg_recv.at[0, 1], partner)]
        for d in range(1, nx):
            xx = xmod(x + d)
            out.append(rcopy(src, lgall.at[x, 0:128], lg_send.at[d, 0], lg_recv.at[d, 0], (xx, r)))
            out.append(
                rcopy(src, lgall.at[x, 128:256], lg_send.at[d, 1], lg_recv.at[d, 1], (xx, chip * 2 + 1 - c))
            )
        return out

    def lg_wait(d, side):
        group = xmod(x - d)
        slot = lgall.at[group, 128 * side:128 * side + 128]
        rcopy(slot, slot, lg_send.at[d, side], lg_recv.at[d, side], partner).wait_recv()

    for copy in lg_copies():
        copy.start()
    crossed = jnp.sum(target * d_logits, axis=1, keepdims=True)
    crs[...] = jnp.broadcast_to(crossed, (128, 128)).T[0:8, :]

    def cr_copy(d):
        return rcopy(crs, crsr.at[d - 1], cr_send.at[d - 1], cr_recv.at[d - 1], (xmod(x + d), r))

    for d in range(1, nx):
        cr_copy(d).start()

    lg_wait(0, 1)
    lg_t = lgall[x].astype(F32).T.astype(BF16)
    odd = lax.rem(p + q + c, 2)

    def partial(pp, i):
        qq = 2 * i + lax.rem(pp + c, 2)
        lanes = pl.ds(pl.multiple_of(chip_of(pp, qq) * 128, 128), 128)
        return jnp.dot(lg_t, hb[:, lanes], preferred_element_type=F32)

    def rs_copy(d):
        return rcopy(rss.at[d - 1], rsr.at[d - 1], rs_send.at[d - 1], rs_recv.at[d - 1], at(p + d, q))

    for d in sorted(range(1, ring), key=lambda d: -min(d, ring - d)):
        for i in range(half):
            rss[d - 1, i] = partial(mod(p + d), i).astype(BF16)
        rs_copy(d).start()
    for i in range(half):
        rso[i] = partial(p, i)

    loss = covered * (all_dmax + jnp.log(all_dsum))
    loss_row = jnp.broadcast_to(loss, (128, 128)).T[0:8, :] - crs[...]
    for d in range(1, nx):
        cr_copy(d).wait_recv()
        loss_row -= crsr[d - 1]
    loss_ref[...] = loss_row

    for d in range(1, nx):
        for side in (0, 1):
            lg_wait(d, side)

    wide = ring * 128
    piece_wide = part * 128

    def gh_lanes(h, i, xx):
        if i < whole:
            return pl.ds(pl.multiple_of(class_y(h, i) * wide, wide), wide)
        return pl.ds(pl.multiple_of(class_y(h, i) * wide + xx * piece_wide, piece_wide), piece_wide)

    def gh_src(i, side):
        return ghs.at[i, 128 * side:128 * side + 128, 0:wide if i < whole else piece_wide]

    def gh_copies(i):
        lanes = gh_lanes(c, i, x)
        mine = pltpu.make_async_copy(gh_src(i, 0), gh_ref.at[:, lanes], gh_loc.at[i])
        theirs = rcopy(gh_src(i, 1), gh_ref.at[:, lanes], gh_send.at[i], gh_recv.at[i], partner)
        return mine, theirs

    def gx_copies(i):
        out = []
        if nx > 1:
            lanes = gh_lanes(c, i, x)
            for side in (0, 1):
                core = chip * 2 + (c if side == 0 else 1 - c)
                for kind, xx in ((0, xmod(x + 1)), (1, xmod(x - 1))):
                    out.append(
                        rcopy(
                            gh_src(i, side), gh_ref.at[:, lanes], gx_send.at[side, i - whole, kind],
                            gx_recv.at[side, i - whole, kind], (xx, core),
                        )
                    )
        return out

    def gx_arrived(side, i, kind):
        h = c if side == 0 else 1 - c
        xx = {0: xmod(x - 1), 1: xmod(x + 1), 2: xmod(x + 2)}[kind]
        slot = gh_ref.at[:, gh_lanes(h, i, xx)]
        return rcopy(slot, slot, gy_send.at[side, i - whole], gx_recv.at[side, i - whole, kind], (xmod(x + 1), r))

    def gx_relay(side, i):
        kind = (i - whole) % 2
        gx_arrived(side, i, kind).wait_recv()
        h = c if side == 0 else 1 - c
        slot = gh_ref.at[:, gh_lanes(h, i, xmod(x - 1) if kind == 0 else xmod(x + 1))]
        dev = (xmod(x + 1) if kind == 0 else xmod(x - 1), r)
        rcopy(slot, slot, gy_send.at[side, i - whole], gx_recv.at[side, i - whole, 2], dev).start()

    for i in range(whole, half):
        for d in range(nx):
            slot = dq.at[xmod(x - d), i - whole]
            if d == 0:
                @pl.when(c == 1)
                def _():
                    dq_copies(1, i)[0].wait()

                @pl.when(c == 0)
                def _():
                    rcopy(slot, slot, dq_send.at[0, 0, 0], dq_recv.at[0, i - whole], partner).wait_recv()
            else:
                rcopy(slot, slot, dq_send.at[0, 0, 0], dq_recv.at[d, i - whole], partner).wait_recv()

        for s in range(part):
            summed = jnp.zeros((256, 128), F32)
            for g in range(nx):
                piece = lax.dot_general(lgall[g], dq[g, i - whole, s], NT, preferred_element_type=F32)
                summed += piece.astype(BF16).astype(F32)
            ghs[i, :, 128 * s:128 * s + 128] = summed.astype(BF16)
        for copy in (*gx_copies(i), *gh_copies(i)):
            copy.start()

    for i in range(whole):
        if nx > 1:
            for kind in (0, 1, 2):
                if kind == i % 2:
                    continue
                x_arrived(kind, i).wait_recv()

        @pl.when(c == 0)
        def _():
            x_arrived(3, i).wait_recv()

        @pl.when(c == 1)
        def _():
            pltpu.make_async_copy(wbuf.at[class_y(1, i), :, :, 128:256], dall.at[x, i], xg_recv.at[3, i]).wait()

        def width(s, carry):
            summed = jnp.zeros((256, 128), F32)
            for g in range(nx):
                piece = lax.dot_general(lgall[g], dall[g, i, s], NT, preferred_element_type=F32)
                summed += piece.astype(BF16).astype(F32)
            ghs[i, :, pl.ds(pl.multiple_of(s * 128, 128), 128)] = summed.astype(BF16)
            return carry

        lax.fori_loop(0, ring, width, 0)
        for copy in gh_copies(i):
            copy.start()

    for d in range(1, ring):
        rs_copy(d).wait_recv()

    def add_up(i, carry):
        total = rso[i]
        for d in range(1, ring):
            total += rsr[d - 1, i].astype(F32)
        fsd[i] = total.T.astype(BF16)
        return carry

    lax.fori_loop(0, half, add_up, 0)

    def f_copy(i, core):
        d = odd + 2 * i
        qq = mod(q + d)
        j = (qq - lax.rem(p + c, 2)) // 2
        dev = (x, chip_of(p, qq) * 2 + core)
        return rcopy(
            fsd.at[j, 64 * core:64 * core + 64], fin.at[d], f_send.at[i, core], f_recv.at[d], dev
        )

    def f_stays(i, core):
        return jnp.logical_and(odd + 2 * i == 0, core == c)

    for i in range(half):
        for core in (0, 1):
            stays = f_stays(i, core)

            @pl.when(jnp.logical_not(stays))
            def _():
                f_copy(i, core).start()

            @pl.when(stays)
            def _():
                j = (q - lax.rem(p + c, 2)) // 2
                fin[0] = fsd[j, 64 * core:64 * core + 64, :]

    if nx == 4:
        for i in range(whole, half):
            for side in (0, 1):
                gx_relay(side, i)

    home = lax.rem(y + z + c, 2) == 0
    grad = jnp.zeros((64, 128), F32)
    for d in range(ring):
        slot = fin.at[d]
        arrival = rcopy(slot, slot, f_send.at[0, 0], f_recv.at[d], partner)
        if d == 0:
            pl.when(jnp.logical_not(home))(arrival.wait_recv)
        else:
            arrival.wait_recv()
        grad += fin[d].astype(F32)
    gd_ref[...] = grad

    for i in range(half):
        mine, theirs = gh_copies(i)
        mine.wait()
        theirs.wait_send()
    for i in range(half):
        slot = gh_ref.at[:, gh_lanes(1 - c, i, x)]
        rcopy(slot, slot, gh_send.at[i], gh_recv.at[i], partner).wait_recv()
    if nx == 4:
        for i in range(whole, half):
            for side in (0, 1):
                for kind in (0, 1, 2):
                    if kind != (i - whole) % 2:
                        gx_arrived(side, i, kind).wait_recv()
                gx_arrived(side, i, 0).wait_send()
            for copy in gx_copies(i):
                copy.wait_send()
    for i in range(half):
        for core in (0, 1):
            @pl.when(jnp.logical_not(f_stays(i, core)))
            def _():
                f_copy(i, core).wait_send()
    for d in range(1, ring):
        rs_copy(d).wait_send()
    for d in range(1, nx):
        cr_copy(d).wait_send()
        sm_copy(d).wait_send()
        st_copy(d).wait_send()
    for copy in lg_copies():
        copy.wait_send()
    lx.wait_send()
    hid_out.wait_send()

    @pl.when(c == 0)
    def _():
        to_b1.wait_send()
        to_b2.wait_send()

    @pl.when(c == 1)
    def _():
        to_a.wait_send()
        for h in (0, 1):
            for i in range(whole):
                for n, copy in enumerate(x_copies(h, i)):
                    if nx > 1 and n < 2 or h == 0:
                        copy.wait_send()
            for i in range(whole, half):
                for d, copy in enumerate(dq_copies(h, i)):
                    if d > 0 or h == 0:
                        copy.wait_send()

    if nx == 4:
        for i in range(whole):
            x_arrived(0, i).wait_send()
    for n, event in enumerate(events):
        for net in (0, 1):
            slab = half_slab(net, (0, 0))
            rcopy(slab, slab, ag_send.at[net, n], ag_recv.at[net, n], partner).wait_send()


def deliver(tiles, loss_in, gh_in, gd_in, loss_out, gh_out, gd_out, wide_loss, loss_buf, gh_buf, gd_buf, come, go):
    rows = gh_in.shape[0] // CHUNKS
    chunks = [slice(rows * n, rows * n + rows) for n in range(CHUNKS)]
    take_loss = pltpu.make_async_copy(loss_in, wide_loss, come.at[CHUNKS])
    take_gd = pltpu.make_async_copy(gd_in, gd_buf, come.at[CHUNKS + 1])
    put_loss = pltpu.make_async_copy(loss_buf, loss_out, go.at[CHUNKS])
    put_gd = pltpu.make_async_copy(gd_buf, gd_out, go.at[CHUNKS + 1])
    take = [pltpu.make_async_copy(gh_in.at[k], gh_buf.at[k], come.at[n]) for n, k in enumerate(chunks)]
    put = [pltpu.make_async_copy(gh_buf.at[k], gh_out.at[k], go.at[n]) for n, k in enumerate(chunks)]
    for copy in (take_loss, take_gd, *take):
        copy.start()
    take_loss.wait()
    lanes = loss_buf.shape[1]
    for t in range(tiles):
        loss_buf[t:t + 1, :] = wide_loss[0:1, lanes * t:lanes * t + lanes]
    put_loss.start()
    take_gd.wait()
    put_gd.start()
    for taken, given in zip(take, put):
        taken.wait()
        given.start()
    for copy in (put_loss, put_gd, *put):
        copy.wait()


def per_device(nx, ring, hidden, teacher_weight, draft_weight, draft_list):
    tiles, tile_rows, width = hidden.shape
    rows = tiles * tile_rows
    half = ring // 2
    whole = half // 2
    parts = half - whole
    dma = pltpu.SemaphoreType.DMA
    more = max(nx - 1, 1)
    scratch = [
        pltpu.VMEM((ring, ring, 128, 256), BF16),
        pltpu.VMEM((2 * rows, width), BF16),
        pltpu.VMEM((2 * rows, 256), F32),
        pltpu.VMEM((rows, 512), F32),
        pltpu.VMEM((nx, max(whole, 1), ring, 128, 128), BF16),
        pltpu.VMEM((nx, half - whole, ring // nx, 128, 128), BF16),
        pltpu.VMEM((more, rows, 128), BF16),
        pltpu.VMEM((more, rows, 128), BF16),
        pltpu.VMEM((8, 128), F32),
        pltpu.VMEM((more, 8, 128), F32),
        pltpu.VMEM((rows, 128), F32),
        pltpu.VMEM((nx, 2 * rows, 128), BF16),
        pltpu.VMEM((8, 128), F32),
        pltpu.VMEM((more, 8, 128), F32),
        pltpu.VMEM((ring - 1, half, 128, 128), BF16),
        pltpu.VMEM((ring - 1, half, 128, 128), BF16),
        pltpu.VMEM((half, 128, 128), F32),
        pltpu.VMEM((half, 128, 128), BF16),
        pltpu.VMEM((ring, 64, 128), BF16),
        pltpu.VMEM((half, 2 * rows, ring * 128), BF16),
        dma((6,)), dma((3,)), dma((2, ring * ring)), dma((2, ring * ring)),
        dma((2, half, 3)), dma((4, half)), dma((half,)), dma((2, parts, nx)), dma((nx, parts)),
        dma(()), dma(()), dma((more,)), dma((more,)), dma((more,)), dma((more,)),
        dma((nx, 2)), dma((nx, 2)), dma((more,)), dma((more,)),
        dma((ring - 1,)), dma((ring - 1,)), dma((half, 2)), dma((ring,)),
        dma((half,)), dma((half,)), dma((half,)),
        dma((2, parts, 2)), dma((2, parts, 3)), dma((2, parts)),
    ]
    hbm = pl.BlockSpec(memory_space=pl.ANY)
    vmem = pl.BlockSpec(memory_space=pltpu.VMEM)
    loss, grad_hidden, grad_draft = pl.pallas_call(
        functools.partial(kernel, nx, ring),
        out_shape=(
            jax.ShapeDtypeStruct((8, 128), F32),
            jax.ShapeDtypeStruct((rows, width), BF16),
            jax.ShapeDtypeStruct((64, 128), F32),
        ),
        in_specs=[pl.BlockSpec(memory_space=pltpu.SMEM), hbm, hbm, hbm],
        out_specs=(vmem, hbm, vmem),
        scratch_shapes=scratch,
        compiler_params=pltpu.CompilerParams(
            collective_id=0, has_side_effects=True, vmem_limit_bytes=60 * 1024 * 1024
        ),
        name="distill",
    )(draft_list, hidden.reshape(rows, width), teacher_weight, draft_weight)
    loss, grad_hidden, grad_draft = pl.pallas_call(
        functools.partial(deliver, tiles),
        out_shape=(
            jax.ShapeDtypeStruct((tiles, tile_rows), F32),
            jax.ShapeDtypeStruct((rows, width), BF16),
            jax.ShapeDtypeStruct((64, 128), F32),
        ),
        in_specs=[hbm, hbm, hbm],
        out_specs=(hbm, hbm, hbm),
        scratch_shapes=[
            pltpu.VMEM((8, 128), F32), pltpu.VMEM((tiles, tile_rows), F32), pltpu.VMEM((rows, width), BF16),
            pltpu.VMEM((64, 128), F32), dma((CHUNKS + 2,)), dma((CHUNKS + 2,)),
        ],
        compiler_params=pltpu.CompilerParams(vmem_limit_bytes=60 * 1024 * 1024),
        name="deliver",
    )(loss, grad_hidden, grad_draft)
    return loss, grad_hidden.reshape(hidden.shape), grad_draft


def solution(mesh):
    nx, devices = mesh.shape["vocab"], mesh.shape["rows"]
    ring = int(round((devices // 2) ** 0.5))
    in_specs = (P(None, "rows", None), P("rows", "vocab"), P("rows", "vocab"), P())
    out_specs = (P(None, "rows"), P(None, "rows", None), P("rows", "vocab"))
    return jax.shard_map(
        functools.partial(per_device, nx, ring), mesh=mesh, in_specs=in_specs, out_specs=out_specs, check_vma=False
    )
```
